32 devices in a mesh: dp: 8 (over z, x), mp: 4 (over y, core).
Axes of the slice: x: 2, y: 2, z: 4, core: 2. Of those that a mesh axis runs over, the one named last changes fastest.
Arguments:
- hidden: bfloat16 [1280, 4096], P('mp', 'dp'), may hold values from -6 to 6
- qkv: bfloat16 [3, 1280, 4096], P(None, 'mp', 'dp'), may hold values from -18 to 18
- helper: int32 [64, 1], P('dp'), may hold values from 0 to 7; in each aligned block of 8 rows (0 to 7, 8 to 15, ...) no two rows name the same one
- segments: int32 [64, 64], P('dp'), may hold values from 0 to 1, as said below
- grad_attn: bfloat16 [1280, 4096], P('mp', 'dp'), may hold values from -6 to 6
Outputs:
- token_grads: bfloat16 [3, 1280, 4096], P(None, 'mp', 'dp')
- weight_grad: float32 [1280, 3, 1280], P('dp', None, 'mp')
The draws below stay inside these ranges and needn't reach their ends.
Inputs may be any that keep to these rules, and one draw needn't show every extreme that they name: Among the 8 windows of one index of dp no helper is named more than 1 times, a bound that some block reaches. `segments`: within each slot the video number starts at 0 and steps at most once to 1, with 16 or more patches on each side of the step.
All inputs are finite; a program needn't handle non-finite values.
Results may differ from the reference program's by a relative error of at most 0.0095.
Values may be sent and summed in bfloat16 or wider, within the bound.
A program may use at most 64 MiB of HBM per device.

```python
import math
import jax
import jax.numpy as jnp
import numpy as np
from jax import lax

D = 1280
HEADS = 16
HEAD_DIM = 80
WIN = 64
BLK_DEV = 8
CAP = 1
BLOCKS = 64
TOKENS = 4096
SLOTS = 64
N_DP = 8


def draw_qkv(key, part):
    first = jax.random.fold_in(jax.random.fold_in(key, 17), 0)
    base = jnp.clip(jax.random.normal(first, (TOKENS, 3, D), jnp.float32), -3.0, 3.0)
    return jnp.transpose(base, (1, 2, 0)).astype(jnp.bfloat16)


def draw_segments(key, part):
    first, second = jax.random.split(jax.random.fold_in(key, 29))
    cut = jax.random.randint(first, (SLOTS,), 0, 8)
    where = jax.random.randint(second, (SLOTS,), WIN // 4, WIN - WIN // 4 + 1)
    has = (cut == 0) | (jnp.arange(SLOTS) == 0)
    position = jnp.arange(WIN)
    return jnp.where(has[:, None] & (position[None, :] >= where[:, None]), 1, 0).astype(jnp.int32)


def strengthened(entries, own_key, source, target, parts, factor):
    def block_of(dim):
        return (jnp.arange(entries.shape[dim]) // (entries.shape[dim] // parts)).reshape((-1,) + (1,) * (entries.ndim - 1 - dim))

    near = jax.random.permutation(own_key, parts)[block_of(target)]
    second = (block_of(target) + parts // 2) % parts
    return jnp.where((block_of(source) == near) | (block_of(source) == second), factor * entries, entries)


def levels(key, dims, cuts, low, largest):
    factor_of = 1.0
    for dim, shards_of in cuts:
        draws = jax.random.uniform(jax.random.fold_in(jax.random.fold_in(key, 6), dim), (shards_of,), jnp.float32, low / len(cuts), largest / len(cuts))
        factor_of = factor_of * jnp.repeat(jnp.exp(draws), dims[dim] // shards_of).reshape((-1,) + (1,) * (len(dims) - 1 - dim))
    return factor_of


def routed_block(key, own, number, rows, amount, top, most, lean):
    ranking = jax.random.permutation(key, amount)
    heavy_load, common = portions_of(amount, rows * top, most, lean, True), portions_of(amount, rows * top, most, lean, False)
    places = jnp.arange(amount)

    def named(tallies, turn):
        used = int((tallies > 0).sum())
        fixed = max(1, used // 4)
        passed = fixed + (places - fixed + turn * (used - fixed)) % max(1, amount - fixed)
        return jnp.zeros((amount,), jnp.int32).at[ranking[jnp.where(places < fixed, places, passed)]].set(jnp.asarray(tallies, jnp.int32))

    tallies = jnp.where(number % 4 == 0, named(heavy_load, number // 4), named(common, number - number // 4 - 1))
    mixed = jax.random.permutation(jax.random.fold_in(own, 3), amount)
    donor, taker = mixed[0:amount // 2 * 2:2], mixed[1:amount // 2 * 2:2]
    slack = jnp.minimum(tallies[donor] - 1, most - tallies[taker]) // 2
    slack = jnp.where((donor == ranking[0]) | (taker == ranking[0]) | (tallies[taker] == 0), 0, jnp.maximum(slack, 0))
    passed = jax.random.randint(jax.random.fold_in(own, 4), (amount // 2,), 0, 1 << 20) % (slack + 1)
    tallies = tallies.at[donor].add(-passed).at[taker].add(passed)
    items = jnp.searchsorted(jnp.cumsum(tallies), jnp.arange(rows * top), side="right").astype(jnp.int32)
    grid = items.reshape(top, rows).T
    grid = grid[jax.random.permutation(jax.random.fold_in(own, 1), rows)]
    turn = jax.random.randint(jax.random.fold_in(own, 2), (rows, 1), 0, top)
    return jnp.take_along_axis(grid, (jnp.arange(top)[None, :] + turn) % top, axis=1)


def portions_of(number_of, total, limit, skew, full):
    weights = [(1 << 20) // math.isqrt(standing ** skew) + 1 for standing in range(1, number_of + 1)]
    largest = limit if full else min(limit, max(-(-total // number_of), total * weights[0] // sum(weights)))
    least = 1 if total - largest >= number_of - 1 else 0
    holding, spare = [largest] + [least] * (number_of - 1), total - largest - least * (number_of - 1)
    while spare > 0:
        free = [i for i in range(1, number_of) if holding[i] < largest] or [i for i in range(1, number_of) if holding[i] < limit]
        pool, budget = sum([weights[i] for i in free]), spare
        for i in free:
            addition = min(limit - holding[i], max(1, budget * weights[i] // pool), spare)
            holding[i] = holding[i] + addition
            spare = spare - addition
    return np.array(holding)


def gaussian(stream_key, dims, deviation, reach, shards=(), kind=jnp.bfloat16):
    drawn = deviation * jax.random.normal(stream_key, dims, jnp.float32)
    if shards:
        drawn = drawn * levels(stream_key, dims, shards, -0.22, 0.18)
    return jnp.clip(drawn, -reach, reach).astype(kind)


def noise_with(key, extent, deviation, reach, cuts, heavy, kind=jnp.bfloat16):
    values = deviation * jax.random.normal(key, extent, jnp.float32)
    if cuts:
        values = values * levels(key, extent, cuts, -0.22, 0.18)
    return jnp.clip(strengthened(values, jax.random.fold_in(key, 3), *heavy), -reach, reach).astype(kind)


def setup_inputs(seed: int = 0) -> dict:
    arg_keys = jax.random.split(jax.random.key(seed), 6)
    hidden = noise_with(arg_keys[0], (D, TOKENS), 1.0, 6.0, ((0, 4), (1, 8)), (1, 0, 8, 2.0))
    qkv = draw_qkv(jax.random.fold_in(arg_keys[5], 71), 0)
    helper_keys = jax.random.split(jax.random.fold_in(arg_keys[2], 1), BLOCKS // BLK_DEV)
    helper_turns = jax.random.permutation(jax.random.fold_in(arg_keys[2], 3), BLOCKS // BLK_DEV)
    helper = jax.vmap(lambda own, number: routed_block(jax.random.fold_in(arg_keys[2], 2), own, number, BLK_DEV, N_DP, 1, CAP, 2))(helper_keys, helper_turns).reshape((BLOCKS, 1))
    segments = draw_segments(jax.random.fold_in(arg_keys[5], 71), 0)
    grad_attn = gaussian(arg_keys[4], (D, SLOTS * WIN), 1.0, 6.0, ((0, 4), (1, 8)))
    return dict(hidden=hidden, qkv=qkv, helper=helper, segments=segments, grad_attn=grad_attn)


def attend_back(query, keys, values, dout, seg):
    scale = 1.0 / math.sqrt(query.shape[-1])
    scores = jnp.einsum('qhe,khe->hqk', query.astype(jnp.float32), keys.astype(jnp.float32)) * scale
    same = seg[:, None] == seg[None, :]
    scores = jnp.where(same[None], scores, -1e+30)
    prob = jnp.exp(scores - lax.optimization_barrier(jnp.max(scores, axis=-1, keepdims=True)))
    prob = prob / lax.optimization_barrier(jnp.sum(prob, axis=-1, keepdims=True))
    probb = prob.astype(jnp.bfloat16)
    attn = jnp.einsum('hqk,khe->qhe', probb.astype(jnp.float32), values.astype(jnp.float32))
    delta = lax.optimization_barrier(jnp.sum(dout.astype(jnp.float32) * attn, axis=-1))
    dvalue = jnp.einsum('hqk,qhe->khe', probb.astype(jnp.float32), dout.astype(jnp.float32)).astype(jnp.bfloat16)
    dprob = jnp.einsum('qhe,khe->hqk', dout.astype(jnp.float32), values.astype(jnp.float32))
    dscore = (prob * (dprob - jnp.transpose(delta)[:, :, None])).astype(jnp.bfloat16)
    dquery = (jnp.einsum('hqk,khe->qhe', dscore.astype(jnp.float32), keys.astype(jnp.float32)) * scale).astype(jnp.bfloat16)
    dkey = (jnp.einsum('hqk,qhe->khe', dscore.astype(jnp.float32), query.astype(jnp.float32)) * scale).astype(jnp.bfloat16)
    return jnp.stack([dquery, dkey, dvalue], axis=1)

def reference(hidden, qkv, helper, segments, grad_attn):
    capacity = max(1, BLK_DEV // N_DP)
    target = helper[:, 0].reshape(N_DP, BLK_DEV)
    onehot = (target[:, :, None] == jnp.arange(N_DP, dtype=jnp.int32)[None, None, :]).astype(jnp.int32)
    rank = lax.optimization_barrier(jnp.sum(onehot * (jnp.cumsum(onehot, axis=1) - 1), axis=2))
    owner = jnp.arange(N_DP, dtype=jnp.int32)[:, None]
    slot = (target * (N_DP * capacity) + owner * capacity + rank).reshape(-1).astype(jnp.int32)
    windows = jnp.transpose(qkv, (2, 0, 1)).reshape(BLOCKS, WIN, 3, HEADS, HEAD_DIM)
    cotangent = jnp.transpose(grad_attn).reshape(SLOTS, WIN, D)

    def one_window(args):
        window, index = args
        seg = segments[index]
        dout = cotangent[index].reshape(WIN, HEADS, HEAD_DIM)
        return attend_back(window[:, 0], window[:, 1], window[:, 2], dout, seg)
    grads = lax.map(one_window, (windows, slot))
    flat = grads.reshape(TOKENS, 3 * D)
    weight_grad = jnp.dot(hidden, flat, preferred_element_type=jnp.float32)
    token_grads = jnp.transpose(grads.reshape(TOKENS, 3, D), (1, 2, 0))
    return (token_grads, weight_grad.reshape(D, 3, D))
```

```python
import functools
import math

import jax
import jax.numpy as jnp
from jax import lax
from jax.experimental import pallas as pl
from jax.experimental.pallas import tpu as pltpu
from jax.sharding import PartitionSpec as P

HEAD_DIM = 80
MESH = pl.DeviceIdType.MESH


def contract(a, b, dims):
    return lax.dot_general(a, b, (dims, ((), ())), preferred_element_type=jnp.float32)


def pieces_of(total):
    lanes = 128
    sizes = [total % lanes] if total % lanes else []
    whole = total // lanes
    if whole > 3:
        sizes += [lanes] * whole
    else:
        sizes += [lanes] * whole
    out, high = [], total
    for size in sizes:
        high -= size
        out.append((high, size))
    return out


def shape_sent(rows, size):
    return (rows // 2, 2 * size) if 2 * size <= 128 and rows % 32 == 0 else (rows, size)


def kernel(n_dp, n_mp, helper_hbm, hid_hbm, qkv_hbm, seg_hbm, ga_hbm, tg_ref, wg_ref,
           helper_ref, seg_ref, hid_ref, qkv_ref, ga_ref, mate_tg,
           seg_send, seg_recv, ga_send, ga_recv, hid_all, prob_s, dout_s, acc, sends, recvs,
           load_sem, seg_ss, seg_rs, ga_ss, ga_rs, hx_ss, hx_rs, hy_ss, hy_rs, hp_ss, hp_rs, own_sem,
           tg_ss, tg_rs, st_ss, st_rs):
    d = lax.axis_index("dp")
    m = lax.axis_index("mp")
    y, c = m // 2, m % 2
    z, x = d // 2, d % 2
    far, groups = n_mp // 2, n_dp // 2
    win = seg_ref.shape[1]
    pair = 2 * win
    width, tokens = qkv_ref.shape[1], qkv_ref.shape[2]
    heads, pairs = width // HEAD_DIM, tokens // pair
    half = width // 2
    blocks, rows = hid_ref.shape[0], hid_ref.shape[2]
    scale = 1.0 / math.sqrt(HEAD_DIM)
    mate = 2 * y + 1 - c
    beside = 2 * z + 1 - x
    pieces = pieces_of(3 * width)
    bits = groups.bit_length() - 1
    bf16, f32 = jnp.bfloat16, jnp.float32

    loads = [pltpu.make_async_copy(a, b, load_sem.at[i])
             for i, (a, b) in enumerate(((ga_hbm, ga_ref), (hid_hbm, hid_ref), (qkv_hbm, qkv_ref),
                                         (seg_hbm, seg_ref), (helper_hbm, helper_ref)))]
    for i in (0, 3, 1, 2, 4):
        loads[i].start()

    barrier = pltpu.get_barrier_semaphore()
    for k in range(1, n_dp):
        pl.semaphore_signal(barrier, inc=1, device_id={"dp": lax.rem(d + k, n_dp)}, device_id_type=MESH)
    for k in range(1, far):
        pl.semaphore_signal(barrier, inc=1, device_id={"mp": 2 * lax.rem(y + k, far) + c}, device_id_type=MESH)
    pl.semaphore_signal(barrier, inc=1, device_id={"mp": mate}, device_id_type=MESH)

    loads[0].wait()
    lane = lax.broadcasted_iota(jnp.int32, (half, pair), 1)
    low = lane < win
    for j in range(n_dp // 2):
        both = ga_ref[:, j * pair:(j + 1) * pair].astype(f32)
        top, bottom = both[:half], both[half:]
        ga_send[2 * j] = jnp.where(low, top, pltpu.roll(bottom, win, 1)).astype(bf16)
        ga_send[2 * j + 1] = jnp.where(low, pltpu.roll(top, win, 1), bottom).astype(bf16)
    ga_recv[d] = ga_send[d]
    loads[3].wait()
    seg = seg_ref[...]
    seg_twice = jnp.concatenate([seg, seg], axis=1)
    for o in range(n_dp):
        seg_send[o] = seg_twice[o:o + 1]
    seg_recv[d] = seg_send[d]
    loads[1].wait()

    def seg_copy(k):
        to = lax.rem(d + k, n_dp)
        return pltpu.make_async_remote_copy(seg_send.at[to], seg_recv.at[d], seg_ss.at[k], seg_rs.at[k],
                                            device_id={"dp": to}, device_id_type=MESH)

    def ga_copy(k):
        to = lax.rem(d + k, n_dp)
        return pltpu.make_async_remote_copy(ga_send.at[to], ga_recv.at[d], ga_ss.at[k], ga_rs.at[k],
                                            device_id={"dp": to}, device_id_type=MESH)

    def hid_at(side, member):
        return hid_all.at[side, pl.ds(member * blocks, blocks)]

    own = pltpu.make_async_copy(hid_ref.at[:, x], hid_at(0, m), own_sem)
    hid_x = pltpu.make_async_remote_copy(hid_ref.at[:, 1 - x], hid_at(1, m), hx_ss, hx_rs,
                                         device_id={"dp": beside}, device_id_type=MESH)

    def hid_copy(side, k):
        src = hid_ref.at[:, x] if side == 0 else hid_at(1, m)
        return pltpu.make_async_remote_copy(src, hid_at(side, m), hy_ss.at[side, k], hy_rs.at[side, k],
                                            device_id={"mp": 2 * lax.rem(y + k, far) + c}, device_id_type=MESH)

    def mate_copy(side, k):
        at = hid_at(side, 2 * lax.rem(y - k + far, far) + c)
        src = hid_ref.at[:, x] if (side, k) == (0, 0) else at
        return pltpu.make_async_remote_copy(src, at, hp_ss.at[side, k], hp_rs.at[side, k],
                                            device_id={"mp": mate}, device_id_type=MESH)

    pl.semaphore_wait(barrier, n_dp - 1 + far)
    for k in range(1, n_dp):
        seg_copy(k).start()
    for k in range(2, n_dp, 2):
        ga_copy(k).start()
    hid_x.start()
    for k in range(1, n_dp, 2):
        ga_copy(k).start()
    for k in range(1, far):
        hid_copy(0, k).start()
    mate_copy(0, 0).start()
    own.start()
    loads[2].wait()
    loads[4].wait()

    def at_of(p, h):
        return slice(h * HEAD_DIM, (h + 1) * HEAD_DIM), slice(p * pair, (p + 1) * pair)

    for p in range(pairs):
        for h in range(heads):
            at = at_of(p, h)
            prob_s[p * heads + h] = contract(qkv_ref[(1,) + at], qkv_ref[(0,) + at], ((0,), (0,))) * scale
    for k in range(1, n_dp):
        seg_copy(k).wait()
    lane_row = lax.broadcasted_iota(jnp.int32, (1, pair), 1)
    for p in range(pairs):
        first, second = seg_recv[helper_ref[2 * p]], seg_recv[helper_ref[2 * p + 1]]
        name = jnp.where(lane_row < win, first, second + 2).astype(f32)
        across = jnp.broadcast_to(name, (pair, pair))
        same = across == across.T
        for h in range(heads):
            scores = jnp.where(same, prob_s[p * heads + h], -1e30)
            prob = jnp.exp(scores - jnp.max(scores, axis=0, keepdims=True))
            prob_s[p * heads + h] = prob / jnp.sum(prob, axis=0, keepdims=True)

    hid_x.wait()
    for k in range(1, far):
        hid_copy(1, k).start()
    mate_copy(1, 0).start()
    for k in range(1, far):
        hid_copy(0, k).wait()
        mate_copy(0, k).start()
    for k in range(1, n_dp):
        ga_copy(k).wait()

    def tg_copy(s):
        at = pl.ds(*pieces[s])
        return pltpu.make_async_remote_copy(tg_ref.at[at], mate_tg.at[at], tg_ss.at[s], tg_rs.at[s],
                                            device_id={"dp": beside}, device_id_type=MESH)

    def put(j, p, h, grads):
        tg_ref[j * width + h * HEAD_DIM:j * width + (h + 1) * HEAD_DIM, p * pair:(p + 1) * pair] = grads.astype(bf16)

    for p in range(pairs):
        first = ga_recv[helper_ref[2 * p]].astype(f32)
        second = ga_recv[helper_ref[2 * p + 1]].astype(f32)
        top = jnp.where(low, first, pltpu.roll(second, win, 1))
        bottom = jnp.where(low, pltpu.roll(first, win, 1), second)
        dout_s[:, p * pair:(p + 1) * pair] = jnp.concatenate([top, bottom], axis=0).astype(bf16)
        for h in range(heads):
            put(2, p, h, contract(dout_s[at_of(p, h)], prob_s[p * heads + h].astype(bf16), ((1,), (1,))))
    early = [s for s, (start, _) in enumerate(pieces) if start >= 2 * width]
    for s in early:
        tg_copy(s).start()
    for p in range(pairs):
        if p == pairs // 2:
            for k in range(1, far):
                hid_copy(1, k).wait()
                mate_copy(1, k).start()
        for h in range(heads):
            at = at_of(p, h)
            query, key, value = qkv_ref[(0,) + at], qkv_ref[(1,) + at], qkv_ref[(2,) + at]
            prob = prob_s[p * heads + h]
            dprob = contract(value, dout_s[at], ((0,), (0,)))
            delta = jnp.sum(prob.astype(bf16).astype(f32) * dprob, axis=0, keepdims=True)
            dscore = (prob * (dprob - delta)).astype(bf16)
            put(0, p, h, contract(key, dscore, ((1,), (0,))) * scale)
            put(1, p, h, contract(query, dscore, ((1,), (1,))) * scale)
    for s in range(len(pieces)):
        if s not in early:
            tg_copy(s).start()

    own.wait()
    for side in range(2):
        for k in range(far):
            mate_copy(side, k).wait()

    def terms(s):
        at = slice(pieces[s][0], pieces[s][0] + pieces[s][1])
        if rows % 16 == 0:
            mine, theirs = [hid_all[side].reshape(groups * rows, tokens) for side in range(2)]
            sums = contract(mine, tg_ref[at], ((1,), (1,))) + contract(theirs, mate_tg[at], ((1,), (1,)))
            acc[s][...] = sums.reshape(groups, rows, pieces[s][1])
        else:
            for t in range(groups):
                acc[s][t] = (contract(hid_all[0, t], tg_ref[at], ((1,), (1,)))
                             + contract(hid_all[1, t], mate_tg[at], ((1,), (1,))))

    def half_copy(s, b):
        bit = z // 2 ** b % 2
        to = z + (1 - 2 * bit) * 2 ** b
        return pltpu.make_async_remote_copy(sends[s][b], recvs[s][b], st_ss.at[s, b], st_rs.at[s, b],
                                            device_id={"dp": 2 * to + x}, device_id_type=MESH)

    def begin(s, b):
        bit = z // 2 ** b % 2
        for i in range(groups >> (b + 1)):
            t = z % 2 ** b + (1 - bit) * 2 ** b + i * 2 ** (b + 1)
            block = acc[s][t]
            if sends[s][b].shape[1] != rows:
                block = jnp.concatenate([block[:rows // 2], block[rows // 2:]], axis=1)
            sends[s][b][i] = block.astype(bf16)
        half_copy(s, b).start()

    def end(s, b):
        half_copy(s, b).wait()
        bit = z // 2 ** b % 2
        for i in range(groups >> (b + 1)):
            t = z % 2 ** b + bit * 2 ** b + i * 2 ** (b + 1)
            block = recvs[s][b][i].astype(f32)
            if recvs[s][b].shape[1] != rows:
                block = jnp.concatenate([block[:, :pieces[s][1]], block[:, pieces[s][1]:]], axis=0)
            acc[s][t] = acc[s][t] + block

    def finish(s):
        start, size = pieces[s]
        total = acc[s][z]
        for j in range(3):
            a, b = max(start, j * width), min(start + size, (j + 1) * width)
            if a < b:
                wg_ref[j, :, a - j * width:b - j * width] = total[:, a - start:b - start]

    for turn in range(len(pieces) + 3 * bits):
        if turn < len(pieces):
            tg_copy(turn).wait()
            terms(turn)
            begin(turn, 0)
        for b in range(bits):
            s = turn - 2 - 3 * b
            if 0 <= s < len(pieces):
                end(s, b)
                if b + 1 < bits:
                    begin(s, b + 1)
                else:
                    finish(s)


def write_out(tg_ref, wg_ref, tg_hbm, wg_hbm, sems):
    copies = [pltpu.make_async_copy(tg_ref, tg_hbm, sems.at[0]), pltpu.make_async_copy(wg_ref, wg_hbm, sems.at[1])]
    for copy in copies:
        copy.start()
    for copy in copies:
        copy.wait()


def per_device(n_dp, n_mp, hidden, qkv, helper, segments, grad_attn):
    width, tokens = qkv.shape[1], qkv.shape[2]
    rows = hidden.shape[0] * n_mp // n_dp
    win = segments.shape[1]
    pair = 2 * win
    heads, pairs, groups, far = width // HEAD_DIM, tokens // pair, n_dp // 2, n_mp // 2
    bf16, f32 = jnp.bfloat16, jnp.float32
    vmem, anywhere = pl.BlockSpec(memory_space=pltpu.VMEM), pl.BlockSpec(memory_space=pltpu.HBM)
    dma = pltpu.SemaphoreType.DMA
    pieces = pieces_of(3 * width)
    bits = groups.bit_length() - 1
    halves = [[pltpu.VMEM((groups >> (b + 1),) + shape_sent(rows, size), bf16) for b in range(bits)] for _, size in pieces]
    split = hidden.reshape(-1, 2, rows, tokens)
    token_grads, weight_grad = pl.pallas_call(
        functools.partial(kernel, n_dp, n_mp),
        out_shape=(
            pltpu.VMEM((3 * width, tokens), bf16),
            pltpu.VMEM((3, rows, width), f32),
        ),
        in_specs=[anywhere] * 5,
        out_specs=(vmem, vmem),
        scratch_shapes=[
            pltpu.SMEM(helper.shape[:1], jnp.int32),
            pltpu.VMEM(segments.shape, jnp.int32),
            pltpu.VMEM(split.shape, bf16),
            pltpu.VMEM(qkv.shape, bf16),
            pltpu.VMEM(grad_attn.shape, bf16),
            pltpu.VMEM((3 * width, tokens), bf16),
            pltpu.VMEM((n_dp, 1, pair), jnp.int32),
            pltpu.VMEM((n_dp, 1, pair), jnp.int32),
            pltpu.VMEM((n_dp, width // 2, pair), bf16),
            pltpu.VMEM((n_dp, width // 2, pair), bf16),
            pltpu.VMEM((2, groups, rows, tokens), bf16),
            pltpu.VMEM((pairs * heads, pair, pair), f32),
            pltpu.VMEM((width, tokens), bf16),
            [pltpu.VMEM((groups, rows, size), f32) for _, size in pieces],
            halves,
            halves,
            dma((5,)),
            dma((n_dp,)), dma((n_dp,)), dma((n_dp,)), dma((n_dp,)),
            dma, dma, dma((2, far)), dma((2, far)), dma((2, far)), dma((2, far)), dma,
            dma((len(pieces),)), dma((len(pieces),)), dma((len(pieces), bits)), dma((len(pieces), bits)),
        ],
        compiler_params=pltpu.CompilerParams(
            collective_id=0, has_side_effects=True, vmem_limit_bytes=65000000
        ),
    )(helper[:, 0], split, qkv, segments, grad_attn)
    token_grads, weight_grad = pl.pallas_call(
        write_out,
        out_shape=(
            jax.ShapeDtypeStruct(token_grads.shape, bf16),
            jax.ShapeDtypeStruct(weight_grad.shape, f32),
        ),
        in_specs=[vmem, vmem],
        out_specs=(anywhere, anywhere),
        scratch_shapes=[dma((2,))],
        compiler_params=pltpu.CompilerParams(vmem_limit_bytes=8 * 1024 * 1024),
    )(token_grads, weight_grad)
    return token_grads.reshape(qkv.shape), jnp.transpose(weight_grad, (1, 0, 2))


def solution(mesh):
    in_specs = (P("mp", "dp"), P(None, "mp", "dp"), P("dp", None), P("dp", None), P("mp", "dp"))
    out_specs = (P(None, "mp", "dp"), P("dp", None, "mp"))
    return jax.shard_map(
        functools.partial(per_device, mesh.shape["dp"], mesh.shape["mp"]),
        mesh=mesh, in_specs=in_specs, out_specs=out_specs, check_vma=False,
    )
```

```python
import functools
import math

import jax
import jax.numpy as jnp
from jax import lax
from jax.experimental import pallas as pl
from jax.experimental.pallas import tpu as pltpu
from jax.sharding import PartitionSpec as P

HEAD_DIM = 80
DIRECT_PIECES = 1
MESH = pl.DeviceIdType.MESH


def contract(a, b, dims):
    return lax.dot_general(a, b, (dims, ((), ())), preferred_element_type=jnp.float32)


def parts_of(width):
    return 2 if width // HEAD_DIM % 2 == 0 and width >= 256 else 1


def pieces_of(width):
    lanes, parts = 128, parts_of(width)
    if parts == 1:
        sizes = [3 * width % lanes] * (3 * width % lanes > 0) + [lanes] * (3 * width // lanes)
        out, high = [], 3 * width
        for size in sizes:
            high -= size
            out.append((high, size))
        return out
    upper, lower = [], []
    for j in (2, 1, 0):
        high = (j + 1) * width
        for i in range(width // parts // lanes):
            high -= lanes
            upper += [(high + lanes // 2, lanes // 2), (high, lanes // 2)] if j == 2 and i == 0 else [(high, lanes)]
        while high > j * width:
            size = min(lanes, high - j * width)
            high -= size
            lower.append((high, size))
    return upper + lower


def halved(pieces, parts):
    return pieces[:len(pieces) - DIRECT_PIECES] if parts > 1 else pieces


def shape_sent(rows, size):
    return (rows // 2, 2 * size) if 2 * size <= 128 and rows % 32 == 0 else (rows, size)


def kernel(n_dp, n_mp, helper_hbm, hid_hbm, qkv_hbm, seg_hbm, ga_hbm, tg_ref, wg_ref,
           helper_ref, seg_ref, hid_ref, qkv_ref, ga_ref, mate_tg,
           seg_send, seg_recv, ga_send, ga_recv, hid_all, prob_s, dout_s, acc, sends, recvs, straight_out, straight_in,
           load_sem, seg_ss, seg_rs, ga_ss, ga_rs, hx_ss, hx_rs, hz_ss, hz_rs, hy_ss, hy_rs, hp_ss, hp_rs, own_sem,
           tg_ss, tg_rs, st_ss, st_rs, di_ss, di_rs):
    d = lax.axis_index("dp")
    m = lax.axis_index("mp")
    y, c = m // 2, m % 2
    z, x = d // 2, d % 2
    far, groups = n_mp // 2, n_dp // 2
    win = seg_ref.shape[1]
    pair = 2 * win
    width, tokens = qkv_ref.shape[1], qkv_ref.shape[2]
    heads, pairs = width // HEAD_DIM, tokens // pair
    parts = parts_of(width)
    band = width // parts
    half = band // 2
    blocks, rows = hid_ref.shape[0], hid_ref.shape[2]
    scale = 1.0 / math.sqrt(HEAD_DIM)
    mate = 2 * y + 1 - c
    beside = 2 * z + 1 - x
    pieces = pieces_of(width)
    bits = groups.bit_length() - 1
    bf16, f32 = jnp.bfloat16, jnp.float32

    loads = [pltpu.make_async_copy(a, b, load_sem.at[i])
             for i, (a, b) in enumerate(((ga_hbm, ga_ref), (hid_hbm, hid_ref), (qkv_hbm, qkv_ref),
                                         (seg_hbm, seg_ref), (helper_hbm, helper_ref)))]
    for i in (0, 3, 1, 2, 4):
        loads[i].start()

    barrier = pltpu.get_barrier_semaphore()
    for k in range(1, n_dp):
        pl.semaphore_signal(barrier, inc=1, device_id={"dp": lax.rem(d + k, n_dp)}, device_id_type=MESH)
    for k in range(1, far):
        pl.semaphore_signal(barrier, inc=1, device_id={"mp": 2 * lax.rem(y + k, far) + c}, device_id_type=MESH)
    pl.semaphore_signal(barrier, inc=1, device_id={"mp": mate}, device_id_type=MESH)

    loads[0].wait()
    lane = lax.broadcasted_iota(jnp.int32, (half, pair), 1)
    low = lane < win
    for j in range(n_dp // 2):
        both = ga_ref[:, j * pair:(j + 1) * pair].astype(f32)
        for g in range(parts):
            top, bottom = both[g * band:g * band + half], both[g * band + half:(g + 1) * band]
            ga_send[g, 2 * j] = jnp.where(low, top, pltpu.roll(bottom, win, 1)).astype(bf16)
            ga_send[g, 2 * j + 1] = jnp.where(low, pltpu.roll(top, win, 1), bottom).astype(bf16)
    for g in range(parts):
        ga_recv[g][d] = ga_send[g, d]
    loads[3].wait()
    seg = seg_ref[...]
    seg_twice = jnp.concatenate([seg, seg], axis=1)
    for o in range(n_dp):
        seg_send[o] = seg_twice[o:o + 1]
    seg_recv[d] = seg_send[d]
    loads[1].wait()

    def seg_copy(k):
        to = lax.rem(d + k, n_dp)
        return pltpu.make_async_remote_copy(seg_send.at[to], seg_recv.at[d], seg_ss, seg_rs,
                                            device_id={"dp": to}, device_id_type=MESH)

    others = pl.ds(0, n_dp - 1)
    seg_all = pltpu.make_async_remote_copy(seg_send.at[others], seg_recv.at[others], seg_ss, seg_rs,
                                           device_id={"dp": beside}, device_id_type=MESH)

    def ga_copy(g, k):
        to = lax.rem(d + k, n_dp)
        return pltpu.make_async_remote_copy(ga_send.at[g, to], ga_recv[g].at[d], ga_ss.at[g], ga_rs.at[g],
                                            device_id={"dp": to}, device_id_type=MESH)

    def ga_all(g):
        return pltpu.make_async_remote_copy(ga_send.at[g, others], ga_recv[g].at[others], ga_ss.at[g], ga_rs.at[g],
                                            device_id={"dp": beside}, device_id_type=MESH)

    def hid_at(side, member):
        return hid_all.at[side, pl.ds(member * blocks, blocks)]

    own = pltpu.make_async_copy(hid_ref.at[:, x], hid_at(0, m), own_sem)
    chunks = 5 if rows % 80 == 0 else 1

    def hid_x(q):
        at = pl.ds(q * (rows // chunks), rows // chunks)
        return pltpu.make_async_remote_copy(hid_ref.at[:, 1 - x, at], hid_at(1, m).at[:, at], hx_ss, hx_rs.at[q],
                                            device_id={"dp": beside}, device_id_type=MESH)

    def pass_copy(q, k):
        at = pl.ds(q * (rows // chunks), rows // chunks)
        return pltpu.make_async_remote_copy(hid_at(1, m).at[:, at], hid_at(1, m).at[:, at], hz_ss, hz_rs,
                                            device_id={"mp": 2 * lax.rem(y + k, far) + c}, device_id_type=MESH)

    def hid_copy(k):
        return pltpu.make_async_remote_copy(hid_ref.at[:, x], hid_at(0, m), hy_ss, hy_rs,
                                            device_id={"mp": 2 * lax.rem(y + k, far) + c}, device_id_type=MESH)

    def mate_copy(side, k):
        at = hid_at(side, 2 * lax.rem(y - k + far, far) + c)
        src = hid_ref.at[:, x] if (side, k) == (0, 0) else at
        return pltpu.make_async_remote_copy(src, at, hp_ss.at[side], hp_rs.at[side],
                                            device_id={"mp": mate}, device_id_type=MESH)

    def members(side, count, send, recv):
        at = hid_all.at[side, pl.ds(0, count * blocks)]
        return pltpu.make_async_remote_copy(at, at, send, recv, device_id={"mp": mate}, device_id_type=MESH)

    pl.semaphore_wait(barrier, n_dp - 1 + far)
    for k in range(1, n_dp):
        seg_copy(k).start()
    for k in range(1, far):
        hid_copy(k).start()
    for g in reversed(range(parts)):
        for k in range(1, n_dp):
            ga_copy(g, k).start()
        if g == parts - 1:
            for q in range(chunks):
                hid_x(q).start()
    mate_copy(0, 0).start()
    own.start()
    loads[2].wait()
    loads[4].wait()

    def at_of(p, h):
        return slice(h * HEAD_DIM, (h + 1) * HEAD_DIM), slice(p * pair, (p + 1) * pair)

    for p in range(pairs):
        for h in range(heads):
            at = at_of(p, h)
            prob_s[p * heads + h] = contract(qkv_ref[(1,) + at], qkv_ref[(0,) + at], ((0,), (0,))) * scale
    seg_all.wait()
    lane_row = lax.broadcasted_iota(jnp.int32, (1, pair), 1)
    for p in range(pairs):
        first, second = seg_recv[helper_ref[2 * p]], seg_recv[helper_ref[2 * p + 1]]
        name = jnp.where(lane_row < win, first, second + 2).astype(f32)
        across = jnp.broadcast_to(name, (pair, pair))
        same = across == across.T
        for h in range(heads):
            scores = jnp.where(same, prob_s[p * heads + h], -1e30)
            prob = jnp.exp(scores - jnp.max(scores, axis=0, keepdims=True))
            prob_s[p * heads + h] = prob / jnp.sum(prob, axis=0, keepdims=True)

    def pass_on(q):
        hid_x(q).wait_recv()
        for k in range(1, far):
            pass_copy(q, k).start()

    before = min(2, chunks)
    for q in range(before):
        pass_on(q)

    def tg_copy(s):
        at = pl.ds(*pieces[s])
        return pltpu.make_async_remote_copy(tg_ref.at[at], mate_tg.at[at], tg_ss, tg_rs.at[s],
                                            device_id={"dp": beside}, device_id_type=MESH)

    def put(j, p, h, grads):
        tg_ref[j * width + h * HEAD_DIM:j * width + (h + 1) * HEAD_DIM, p * pair:(p + 1) * pair] = grads.astype(bf16)

    def dv(g, p):
        first = ga_recv[g][helper_ref[2 * p]].astype(f32)
        second = ga_recv[g][helper_ref[2 * p + 1]].astype(f32)
        top = jnp.where(low, first, pltpu.roll(second, win, 1))
        bottom = jnp.where(low, pltpu.roll(first, win, 1), second)
        dout_s[g * band:(g + 1) * band, p * pair:(p + 1) * pair] = jnp.concatenate([top, bottom], axis=0).astype(bf16)
        for h in range(g * heads // parts, (g + 1) * heads // parts):
            put(2, p, h, contract(dout_s[at_of(p, h)], prob_s[p * heads + h].astype(bf16), ((1,), (1,))))

    def attend(g, p):
        for h in range(g * heads // parts, (g + 1) * heads // parts):
            at = at_of(p, h)
            query, key, value = qkv_ref[(0,) + at], qkv_ref[(1,) + at], qkv_ref[(2,) + at]
            prob = prob_s[p * heads + h]
            dprob = contract(value, dout_s[at], ((0,), (0,)))
            delta = jnp.sum(prob.astype(bf16).astype(f32) * dprob, axis=0, keepdims=True)
            dscore = (prob * (dprob - delta)).astype(bf16)
            put(0, p, h, contract(key, dscore, ((1,), (0,))) * scale)
            put(1, p, h, contract(query, dscore, ((1,), (1,))) * scale)

    sent = []

    def send_ready(g, j):
        for s, (start, size) in enumerate(pieces):
            if s not in sent and start // width >= j and (start % width >= g * band or parts == 1 or g == 0):
                if start // width == 2 or j < 2:
                    tg_copy(s).start()
                    sent.append(s)

    later = max(before, chunks - 1)
    for g in reversed(range(parts)):
        ga_all(g).wait()
        for p in range(pairs):
            dv(g, p)
        send_ready(g, 2)
        if g == parts - 1:
            for q in range(before, later):
                pass_on(q)
            members(0, far - 1, hy_ss, hy_rs).wait()
            for k in range(1, far):
                mate_copy(0, k).start()
        for p in range(pairs if g > 0 else 0):
            if p == 1:
                for q in range(later, chunks):
                    pass_on(q)
                mate_copy(1, 0).start()
            attend(g, p)
        if g > 0:
            send_ready(g, 0)
    if parts == 1:
        mate_copy(1, 0).start()
    members(1, far - 1, hz_ss, hz_rs).wait()
    for k in range(1, far):
        mate_copy(1, k).start()
    own.wait()
    members(0, far, hp_ss.at[0], hp_rs.at[0]).wait()

    def products(side, of, s, blocks):
        at = slice(pieces[s][0], pieces[s][0] + pieces[s][1])
        if rows % 16 == 0:
            stacked = jnp.concatenate([hid_all[side, t] for t in blocks], axis=0)
            return contract(stacked, of[at], ((1,), (1,))).reshape(len(blocks), rows, pieces[s][1])
        return [contract(hid_all[side, t], of[at], ((1,), (1,))) for t in blocks]

    def mine(s):
        for t, block in enumerate(products(0, tg_ref, s, range(groups))):
            acc[s][t] = block

    def theirs(s, blocks):
        for t, block in zip(blocks, products(1, mate_tg, s, blocks)):
            acc[s][t] = acc[s][t] + block

    def packed(block):
        if block.shape[1] * 2 <= 128 and rows % 32 == 0:
            block = jnp.concatenate([block[:rows // 2], block[rows // 2:]], axis=1)
        return block.astype(bf16)

    def unpacked(block, size):
        block = block.astype(f32)
        if block.shape[1] != size:
            block = jnp.concatenate([block[:, :size], block[:, size:]], axis=0)
        return block

    def finish(s, total):
        start, size = pieces[s]
        for j in range(3):
            a, b = max(start, j * width), min(start + size, (j + 1) * width)
            if a < b:
                wg_ref[j, :, a - j * width:b - j * width] = total[:, a - start:b - start]

    count = len(pieces)
    straight = len(halved(pieces, parts))
    kinds = sorted({size for _, size in pieces[:straight]})
    place = [(kinds.index(size), sum(other == size for _, other in pieces[:s])) for s, (_, size) in enumerate(pieces[:straight])]

    def outgoing(s, b):
        kind, at = place[s]
        return sends[kind][b].at[at]

    def half_copy(s, b):
        bit = z // 2 ** b % 2
        to = z + (1 - 2 * bit) * 2 ** b
        return pltpu.make_async_remote_copy(outgoing(s, b), recvs[s][b], st_ss.at[place[s][0], b], st_rs.at[s, b],
                                            device_id={"dp": 2 * to + x}, device_id_type=MESH)

    def begin(s, b):
        bit = z // 2 ** b % 2
        for i in range(groups >> (b + 1)):
            t = z % 2 ** b + (1 - bit) * 2 ** b + i * 2 ** (b + 1)
            outgoing(s, b)[i] = packed(acc[s][t])
        half_copy(s, b).start()

    def end(s, b):
        half_copy(s, b).wait_recv()
        bit = z // 2 ** b % 2
        for i in range(groups >> (b + 1)):
            t = z % 2 ** b + bit * 2 ** b + i * 2 ** (b + 1)
            acc[s][t] = acc[s][t] + unpacked(recvs[s][b][i], pieces[s][1])

    def direct_copy(s, k):
        return pltpu.make_async_remote_copy(straight_out.at[s, k - 1], straight_in.at[s, k - 1], di_ss, di_rs,
                                            device_id={"dp": 2 * lax.rem(z + k, groups) + x}, device_id_type=MESH)

    ahead = 2 if parts > 1 else 0
    attends = {2: range(pairs // 2), 3: range(pairs // 2, pairs)} if parts > 1 else {0: range(pairs)}
    for s in range(ahead):
        mine(s)
    members(1, far, hp_ss.at[1], hp_rs.at[1]).wait()
    bit = z % 2
    sent_first = [1 - bit + 2 * i for i in range(groups // 2)]
    kept = [bit + 2 * i for i in range(groups // 2)]
    for turn in range(count + 2 + 4 * (bits - 1)):
        for p in attends.get(turn, ()):
            attend(0, p)
        if turn == max(attends):
            send_ready(0, 0)
        if turn < count:
            if turn >= ahead:
                mine(turn)
            tg_copy(turn).wait_recv()
            if turn < straight:
                theirs(turn, sent_first)
                begin(turn, 0)
                theirs(turn, kept)
            else:
                theirs(turn, range(groups))
                for k in range(1, groups):
                    straight_out[turn - straight, k - 1] = packed(acc[turn][lax.rem(z + k, groups)])
                    direct_copy(turn - straight, k).start()
        for b in range(bits):
            s = turn - 2 - 4 * b
            if 0 <= s < straight:
                end(s, b)
                if b + 1 < bits:
                    begin(s, b + 1)
                else:
                    finish(s, acc[s][z])
    if straight < count:
        pltpu.make_async_remote_copy(straight_out, straight_in, di_ss, di_rs,
                                     device_id={"dp": beside}, device_id_type=MESH).wait()
    for s in range(straight, count):
        total = acc[s][z]
        for k in range(1, groups):
            total = total + unpacked(straight_in[s - straight, k - 1], pieces[s][1])
        finish(s, total)
    pltpu.make_async_remote_copy(tg_ref, mate_tg, tg_ss, tg_rs.at[0],
                                 device_id={"dp": beside}, device_id_type=MESH).wait_send()
    pltpu.make_async_remote_copy(hid_ref.at[:, 1 - x], hid_at(1, m), hx_ss, hx_rs.at[0],
                                 device_id={"dp": beside}, device_id_type=MESH).wait_send()
    for kind in range(len(kinds)):
        for b in range(bits):
            pltpu.make_async_remote_copy(sends[kind][b], sends[kind][b], st_ss.at[kind, b], st_rs.at[0, b],
                                         device_id={"dp": beside}, device_id_type=MESH).wait_send()


def write_out(tg_ref, wg_ref, tg_hbm, wg_hbm, sems):
    copies = [pltpu.make_async_copy(tg_ref, tg_hbm, sems.at[0]), pltpu.make_async_copy(wg_ref, wg_hbm, sems.at[1])]
    for copy in copies:
        copy.start()
    for copy in copies:
        copy.wait()


def per_device(n_dp, n_mp, hidden, qkv, helper, segments, grad_attn):
    width, tokens = qkv.shape[1], qkv.shape[2]
    rows = hidden.shape[0] * n_mp // n_dp
    win = segments.shape[1]
    pair = 2 * win
    parts = parts_of(width)
    heads, pairs, groups, far = width // HEAD_DIM, tokens // pair, n_dp // 2, n_mp // 2
    bf16, f32 = jnp.bfloat16, jnp.float32
    vmem, anywhere = pl.BlockSpec(memory_space=pltpu.VMEM), pl.BlockSpec(memory_space=pltpu.HBM)
    dma = pltpu.SemaphoreType.DMA
    pieces = pieces_of(width)
    bits = groups.bit_length() - 1
    cut = halved(pieces, parts)
    incoming = [[pltpu.VMEM((groups >> (b + 1),) + shape_sent(rows, size), bf16) for b in range(bits)] for _, size in cut]
    kinds = sorted({size for _, size in cut})
    outgoing = [[pltpu.VMEM((sum(size == kind for _, size in cut), groups >> (b + 1)) + shape_sent(rows, kind), bf16)
                 for b in range(bits)] for kind in kinds]
    straight = pltpu.VMEM((max(len(pieces) - len(cut), 1), groups - 1) + shape_sent(rows, pieces[-1][1]), bf16)
    split = hidden.reshape(-1, 2, rows, tokens)
    token_grads, weight_grad = pl.pallas_call(
        functools.partial(kernel, n_dp, n_mp),
        out_shape=(
            pltpu.VMEM((3 * width, tokens), bf16),
            pltpu.VMEM((3, rows, width), f32),
        ),
        in_specs=[anywhere] * 5,
        out_specs=(vmem, vmem),
        scratch_shapes=[
            pltpu.SMEM(helper.shape[:1], jnp.int32),
            pltpu.VMEM(segments.shape, jnp.int32),
            pltpu.VMEM(split.shape, bf16),
            pltpu.VMEM(qkv.shape, bf16),
            pltpu.VMEM(grad_attn.shape, bf16),
            pltpu.VMEM((3 * width, tokens), bf16),
            pltpu.VMEM((n_dp, 1, pair), jnp.int32),
            pltpu.VMEM((n_dp, 1, pair), jnp.int32),
            pltpu.VMEM((parts, n_dp, width // parts // 2, pair), bf16),
            [pltpu.VMEM((n_dp, width // parts // 2, pair), bf16) for _ in range(parts)],
            pltpu.VMEM((2, groups, rows, tokens), bf16),
            pltpu.VMEM((pairs * heads, pair, pair), f32),
            pltpu.VMEM((width, tokens), bf16),
            [pltpu.VMEM((groups, rows, size), f32) for _, size in pieces],
            outgoing,
            incoming,
            straight,
            straight,
            dma((5,)),
            dma, dma, dma((parts,)), dma((parts,)),
            dma, dma((5 if rows % 80 == 0 else 1,)), dma, dma, dma, dma, dma((2,)), dma((2,)), dma,
            dma, dma((len(pieces),)), dma((len(kinds), bits)), dma((len(cut), bits)),
            dma, dma,
        ],
        compiler_params=pltpu.CompilerParams(
            collective_id=0, has_side_effects=True, vmem_limit_bytes=65000000
        ),
    )(helper[:, 0], split, qkv, segments, grad_attn)
    token_grads, weight_grad = pl.pallas_call(
        write_out,
        out_shape=(
            jax.ShapeDtypeStruct(token_grads.shape, bf16),
            jax.ShapeDtypeStruct(weight_grad.shape, f32),
        ),
        in_specs=[vmem, vmem],
        out_specs=(anywhere, anywhere),
        scratch_shapes=[dma((2,))],
        compiler_params=pltpu.CompilerParams(vmem_limit_bytes=8 * 1024 * 1024),
    )(token_grads, weight_grad)
    return token_grads.reshape(qkv.shape), jnp.transpose(weight_grad, (1, 0, 2))


def solution(mesh):
    in_specs = (P("mp", "dp"), P(None, "mp", "dp"), P("dp", None), P("dp", None), P("mp", "dp"))
    out_specs = (P(None, "mp", "dp"), P("dp", None, "mp"))
    return jax.shard_map(
        functools.partial(per_device, mesh.shape["dp"], mesh.shape["mp"]),
        mesh=mesh, in_specs=in_specs, out_specs=out_specs, check_vma=False,
    )
```

```python
import functools
import math

import jax
import jax.numpy as jnp
from jax import lax
from jax.experimental import pallas as pl
from jax.experimental.pallas import tpu as pltpu
from jax.sharding import PartitionSpec as P

HEAD_DIM = 80
DIRECT_PIECES = 1
MESH = pl.DeviceIdType.MESH


def contract(a, b, dims):
    return lax.dot_general(a, b, (dims, ((), ())), preferred_element_type=jnp.float32)


def parts_of(width):
    return 2 if width // HEAD_DIM % 2 == 0 and width >= 256 else 1


def pieces_of(width):
    lanes, parts = 128, parts_of(width)
    if parts == 1:
        sizes = [3 * width % lanes] * (3 * width % lanes > 0) + [lanes] * (3 * width // lanes)
        out, high = [], 3 * width
        for size in sizes:
            high -= size
            out.append((high, size))
        return out
    upper, lower = [], []
    for j in (2, 1, 0):
        high = (j + 1) * width
        for i in range(width // parts // lanes):
            high -= lanes
            upper += [(high + lanes // 2, lanes // 2), (high, lanes // 2)] if j == 2 and i == 0 else [(high, lanes)]
        while high > j * width:
            size = min(lanes, high - j * width)
            high -= size
            lower.append((high, size))
    return upper + lower


def halved(pieces, parts):
    return pieces[:len(pieces) - DIRECT_PIECES] if parts > 1 else pieces


def shape_sent(rows, size):
    return (rows // 2, 2 * size) if 2 * size <= 128 and rows % 32 == 0 else (rows, size)


def kernel(n_dp, n_mp, helper_hbm, hid_hbm, qkv_hbm, seg_hbm, ga_hbm, tg_ref, wg_ref,
           helper_ref, seg_ref, hid_ref, qkv_ref, ga_ref, mate_tg,
           seg_send, seg_recv, ga_send, ga_recv, hid_all, prob_s, dout_s, acc, sends, recvs, straight_out, straight_in,
           load_sem, seg_ss, seg_rs, ga_ss, ga_rs, hx_ss, hx_rs, hz_ss, hz_rs, hy_ss, hy_rs, hp_ss, hp_rs, own_sem,
           tg_ss, tg_rs, st_ss, st_rs, di_ss, di_rs):
    d = lax.axis_index("dp")
    m = lax.axis_index("mp")
    y, c = m // 2, m % 2
    z, x = d // 2, d % 2
    far, groups = n_mp // 2, n_dp // 2
    win = seg_ref.shape[1]
    pair = 2 * win
    width, tokens = qkv_ref.shape[1], qkv_ref.shape[2]
    heads, pairs = width // HEAD_DIM, tokens // pair
    parts = parts_of(width)
    band = width // parts
    half = band // 2
    blocks, rows = hid_ref.shape[0], hid_ref.shape[2]
    scale = 1.0 / math.sqrt(HEAD_DIM)
    mate = 2 * y + 1 - c
    beside = 2 * z + 1 - x
    pieces = pieces_of(width)
    bits = groups.bit_length() - 1
    bf16, f32 = jnp.bfloat16, jnp.float32

    loads = [pltpu.make_async_copy(a, b, load_sem.at[i])
             for i, (a, b) in enumerate(((ga_hbm, ga_ref), (hid_hbm, hid_ref), (qkv_hbm, qkv_ref),
                                         (seg_hbm, seg_ref), (helper_hbm, helper_ref)))]
    for i in (0, 3, 1, 2, 4):
        loads[i].start()

    barrier = pltpu.get_barrier_semaphore()
    for k in range(1, n_dp):
        pl.semaphore_signal(barrier, inc=1, device_id={"dp": lax.rem(d + k, n_dp)}, device_id_type=MESH)
    for k in range(1, far):
        pl.semaphore_signal(barrier, inc=1, device_id={"mp": 2 * lax.rem(y + k, far) + c}, device_id_type=MESH)
    pl.semaphore_signal(barrier, inc=1, device_id={"mp": mate}, device_id_type=MESH)

    loads[0].wait()
    lane = lax.broadcasted_iota(jnp.int32, (half, pair), 1)
    low = lane < win
    for j in range(n_dp // 2):
        both = ga_ref[:, j * pair:(j + 1) * pair].astype(f32)
        for g in range(parts):
            top, bottom = both[g * band:g * band + half], both[g * band + half:(g + 1) * band]
            ga_send[g, 2 * j] = jnp.where(low, top, pltpu.roll(bottom, win, 1)).astype(bf16)
            ga_send[g, 2 * j + 1] = jnp.where(low, pltpu.roll(top, win, 1), bottom).astype(bf16)
    for g in range(parts):
        ga_recv[g][d] = ga_send[g, d]
    loads[3].wait()
    seg = seg_ref[...]
    seg_twice = jnp.concatenate([seg, seg], axis=1)
    for o in range(n_dp):
        seg_send[o] = seg_twice[o:o + 1]
    seg_recv[d] = seg_send[d]
    loads[1].wait()

    def seg_copy(k):
        to = lax.rem(d + k, n_dp)
        return pltpu.make_async_remote_copy(seg_send.at[to], seg_recv.at[d], seg_ss, seg_rs,
                                            device_id={"dp": to}, device_id_type=MESH)

    others = pl.ds(0, n_dp - 1)
    seg_all = pltpu.make_async_remote_copy(seg_send.at[others], seg_recv.at[others], seg_ss, seg_rs,
                                           device_id={"dp": beside}, device_id_type=MESH)

    def ga_copy(g, k):
        to = lax.rem(d + k, n_dp)
        return pltpu.make_async_remote_copy(ga_send.at[g, to], ga_recv[g].at[d], ga_ss.at[g], ga_rs.at[g],
                                            device_id={"dp": to}, device_id_type=MESH)

    def ga_all(g):
        return pltpu.make_async_remote_copy(ga_send.at[g, others], ga_recv[g].at[others], ga_ss.at[g], ga_rs.at[g],
                                            device_id={"dp": beside}, device_id_type=MESH)

    def hid_at(side, member):
        return hid_all.at[side, pl.ds(member * blocks, blocks)]

    own = pltpu.make_async_copy(hid_ref.at[:, x], hid_at(0, m), own_sem)
    chunks = 5 if rows % 80 == 0 else 1

    def hid_x(q):
        at = pl.ds(q * (rows // chunks), rows // chunks)
        return pltpu.make_async_remote_copy(hid_ref.at[:, 1 - x, at], hid_at(1, m).at[:, at], hx_ss, hx_rs.at[q],
                                            device_id={"dp": beside}, device_id_type=MESH)

    def pass_copy(q, k):
        at = pl.ds(q * (rows // chunks), rows // chunks)
        return pltpu.make_async_remote_copy(hid_at(1, m).at[:, at], hid_at(1, m).at[:, at], hz_ss, hz_rs,
                                            device_id={"mp": 2 * lax.rem(y + k, far) + c}, device_id_type=MESH)

    def hid_copy(k):
        return pltpu.make_async_remote_copy(hid_ref.at[:, x], hid_at(0, m), hy_ss, hy_rs,
                                            device_id={"mp": 2 * lax.rem(y + k, far) + c}, device_id_type=MESH)

    def mate_copy(side, k):
        at = hid_at(side, 2 * lax.rem(y - k + far, far) + c)
        src = hid_ref.at[:, x] if (side, k) == (0, 0) else at
        return pltpu.make_async_remote_copy(src, at, hp_ss.at[side], hp_rs.at[side],
                                            device_id={"mp": mate}, device_id_type=MESH)

    def members(side, count, send, recv):
        at = hid_all.at[side, pl.ds(0, count * blocks)]
        return pltpu.make_async_remote_copy(at, at, send, recv, device_id={"mp": mate}, device_id_type=MESH)

    pl.semaphore_wait(barrier, n_dp - 1 + far)
    for k in range(1, n_dp):
        seg_copy(k).start()
    for k in range(1, far):
        hid_copy(k).start()
    for k in range(1, n_dp):
        ga_copy(parts - 1, k).start()
    for q in range(chunks):
        hid_x(q).start()
    mate_copy(0, 0).start()
    own.start()
    loads[2].wait()
    loads[4].wait()

    def at_of(p, h):
        return slice(h * HEAD_DIM, (h + 1) * HEAD_DIM), slice(p * pair, (p + 1) * pair)

    for p in range(pairs):
        for h in range(heads):
            at = at_of(p, h)
            prob_s[p * heads + h] = contract(qkv_ref[(1,) + at], qkv_ref[(0,) + at], ((0,), (0,))) * scale
    seg_all.wait()
    lane_row = lax.broadcasted_iota(jnp.int32, (1, pair), 1)
    for p in range(pairs):
        first, second = seg_recv[helper_ref[2 * p]], seg_recv[helper_ref[2 * p + 1]]
        name = jnp.where(lane_row < win, first, second + 2).astype(f32)
        across = jnp.broadcast_to(name, (pair, pair))
        same = across == across.T
        for h in range(heads):
            scores = jnp.where(same, prob_s[p * heads + h], -1e30)
            prob = jnp.exp(scores - jnp.max(scores, axis=0, keepdims=True))
            prob_s[p * heads + h] = prob / jnp.sum(prob, axis=0, keepdims=True)

    def pass_on(q):
        hid_x(q).wait_recv()
        for k in range(1, far):
            pass_copy(q, k).start()

    before = min(2, chunks)
    for g in range(parts - 1):
        for k in range(1, n_dp):
            ga_copy(g, k).start()
    for q in range(before):
        pass_on(q)

    def tg_copy(s):
        at = pl.ds(*pieces[s])
        return pltpu.make_async_remote_copy(tg_ref.at[at], mate_tg.at[at], tg_ss, tg_rs.at[s],
                                            device_id={"dp": beside}, device_id_type=MESH)

    def put(j, p, h, grads):
        tg_ref[j * width + h * HEAD_DIM:j * width + (h + 1) * HEAD_DIM, p * pair:(p + 1) * pair] = grads.astype(bf16)

    def dv(g, p):
        first = ga_recv[g][helper_ref[2 * p]].astype(f32)
        second = ga_recv[g][helper_ref[2 * p + 1]].astype(f32)
        top = jnp.where(low, first, pltpu.roll(second, win, 1))
        bottom = jnp.where(low, pltpu.roll(first, win, 1), second)
        dout_s[g * band:(g + 1) * band, p * pair:(p + 1) * pair] = jnp.concatenate([top, bottom], axis=0).astype(bf16)
        for h in range(g * heads // parts, (g + 1) * heads // parts):
            put(2, p, h, contract(dout_s[at_of(p, h)], prob_s[p * heads + h].astype(bf16), ((1,), (1,))))

    def attend(g, p):
        for h in range(g * heads // parts, (g + 1) * heads // parts):
            at = at_of(p, h)
            query, key, value = qkv_ref[(0,) + at], qkv_ref[(1,) + at], qkv_ref[(2,) + at]
            prob = prob_s[p * heads + h]
            dprob = contract(value, dout_s[at], ((0,), (0,)))
            delta = jnp.sum(prob.astype(bf16).astype(f32) * dprob, axis=0, keepdims=True)
            dscore = (prob * (dprob - delta)).astype(bf16)
            put(0, p, h, contract(key, dscore, ((1,), (0,))) * scale)
            put(1, p, h, contract(query, dscore, ((1,), (1,))) * scale)

    sent = []

    def send_ready(g, j):
        for s, (start, size) in enumerate(pieces):
            if s not in sent and start // width >= j and (start % width >= g * band or parts == 1 or g == 0):
                if start // width == 2 or j < 2:
                    tg_copy(s).start()
                    sent.append(s)

    later = max(before, chunks - 1)
    for g in reversed(range(parts)):
        ga_all(g).wait()
        for p in range(pairs):
            dv(g, p)
        send_ready(g, 2)
        if g == parts - 1:
            for q in range(before, later):
                pass_on(q)
            members(0, far - 1, hy_ss, hy_rs).wait()
            for k in range(1, far):
                mate_copy(0, k).start()
        for p in range(pairs if g > 0 else 0):
            if p == 1:
                for q in range(later, chunks):
                    pass_on(q)
                mate_copy(1, 0).start()
            attend(g, p)
        if g > 0:
            send_ready(g, 0)
    if parts == 1:
        mate_copy(1, 0).start()
    members(1, far - 1, hz_ss, hz_rs).wait()
    for k in range(1, far):
        mate_copy(1, k).start()
    own.wait()
    members(0, far, hp_ss.at[0], hp_rs.at[0]).wait()

    def products(side, of, s, blocks):
        at = slice(pieces[s][0], pieces[s][0] + pieces[s][1])
        if rows % 16 == 0:
            stacked = jnp.concatenate([hid_all[side, t] for t in blocks], axis=0)
            return contract(stacked, of[at], ((1,), (1,))).reshape(len(blocks), rows, pieces[s][1])
        return [contract(hid_all[side, t], of[at], ((1,), (1,))) for t in blocks]

    def mine(s):
        for t, block in enumerate(products(0, tg_ref, s, range(groups))):
            acc[s][t] = block

    def theirs(s, blocks):
        for t, block in zip(blocks, products(1, mate_tg, s, blocks)):
            acc[s][t] = acc[s][t] + block

    def packed(block):
        if block.shape[1] * 2 <= 128 and rows % 32 == 0:
            block = jnp.concatenate([block[:rows // 2], block[rows // 2:]], axis=1)
        return block.astype(bf16)

    def unpacked(block, size):
        block = block.astype(f32)
        if block.shape[1] != size:
            block = jnp.concatenate([block[:, :size], block[:, size:]], axis=0)
        return block

    def finish(s, total):
        start, size = pieces[s]
        for j in range(3):
            a, b = max(start, j * width), min(start + size, (j + 1) * width)
            if a < b:
                wg_ref[j, :, a - j * width:b - j * width] = total[:, a - start:b - start]

    count = len(pieces)
    straight = len(halved(pieces, parts))
    kinds = sorted({size for _, size in pieces[:straight]})
    place = [(kinds.index(size), sum(other == size for _, other in pieces[:s])) for s, (_, size) in enumerate(pieces[:straight])]

    def outgoing(s, b):
        kind, at = place[s]
        return sends[kind][b].at[at]

    def half_copy(s, b):
        bit = z // 2 ** b % 2
        to = z + (1 - 2 * bit) * 2 ** b
        return pltpu.make_async_remote_copy(outgoing(s, b), recvs[s][b], st_ss.at[place[s][0], b], st_rs.at[s, b],
                                            device_id={"dp": 2 * to + x}, device_id_type=MESH)

    def begin(s, b):
        bit = z // 2 ** b % 2
        for i in range(groups >> (b + 1)):
            t = z % 2 ** b + (1 - bit) * 2 ** b + i * 2 ** (b + 1)
            outgoing(s, b)[i] = packed(acc[s][t])
        half_copy(s, b).start()

    def end(s, b):
        half_copy(s, b).wait_recv()
        bit = z // 2 ** b % 2
        for i in range(groups >> (b + 1)):
            t = z % 2 ** b + bit * 2 ** b + i * 2 ** (b + 1)
            acc[s][t] = acc[s][t] + unpacked(recvs[s][b][i], pieces[s][1])

    def direct_copy(s, k):
        return pltpu.make_async_remote_copy(straight_out.at[s, k - 1], straight_in.at[s, k - 1], di_ss, di_rs,
                                            device_id={"dp": 2 * lax.rem(z + k, groups) + x}, device_id_type=MESH)

    def advance(s, b):
        if 0 <= s < straight:
            end(s, b)
            if b + 1 < bits:
                begin(s, b + 1)
            else:
                finish(s, acc[s][z])

    swapped = groups == 4
    inner = z == 2
    ahead = 2 if parts > 1 else 0
    attends = {2: range(pairs // 2), 3: range(pairs // 2, pairs)} if parts > 1 else {0: range(pairs)}
    for s in range(ahead):
        mine(s)
    members(1, far, hp_ss.at[1], hp_rs.at[1]).wait()
    bit = z % 2
    sent_first = [1 - bit + 2 * i for i in range(groups // 2)]
    kept = [bit + 2 * i for i in range(groups // 2)]
    for turn in range(count + 2 + 4 * (bits - 1)):
        for p in attends.get(turn, ()):
            attend(0, p)
        if turn == max(attends):
            send_ready(0, 0)
        if turn < count:
            if turn >= ahead:
                mine(turn)
            tg_copy(turn).wait_recv()
            if turn < straight:
                theirs(turn, sent_first)
                if swapped:
                    pl.when(inner)(functools.partial(advance, turn - 2, 0))
                begin(turn, 0)
                theirs(turn, kept)
            else:
                theirs(turn, range(groups))
                for i in range(groups - 1):
                    t = i + (i >= z).astype(jnp.int32)
                    k = lax.rem(t - z + groups, groups)
                    straight_out[turn - straight, k - 1] = packed(acc[turn][t])
                    direct_copy(turn - straight, k).start()
        for b in range(bits):
            step = functools.partial(advance, turn - 2 - 3 * b, b)
            if swapped and b == 0 and turn < straight:
                pl.when(jnp.logical_not(inner))(step)
            else:
                step()
    if straight < count:
        pltpu.make_async_remote_copy(straight_out, straight_in, di_ss, di_rs,
                                     device_id={"dp": beside}, device_id_type=MESH).wait()
    for s in range(straight, count):
        total = acc[s][z]
        for k in range(1, groups):
            total = total + unpacked(straight_in[s - straight, k - 1], pieces[s][1])
        finish(s, total)
    pltpu.make_async_remote_copy(tg_ref, mate_tg, tg_ss, tg_rs.at[0],
                                 device_id={"dp": beside}, device_id_type=MESH).wait_send()
    pltpu.make_async_remote_copy(hid_ref.at[:, 1 - x], hid_at(1, m), hx_ss, hx_rs.at[0],
                                 device_id={"dp": beside}, device_id_type=MESH).wait_send()
    for kind in range(len(kinds)):
        for b in range(bits):
            pltpu.make_async_remote_copy(sends[kind][b], sends[kind][b], st_ss.at[kind, b], st_rs.at[0, b],
                                         device_id={"dp": beside}, device_id_type=MESH).wait_send()


def write_out(tg_ref, wg_ref, tg_hbm, wg_hbm, sems):
    copies = [pltpu.make_async_copy(tg_ref, tg_hbm, sems.at[0]), pltpu.make_async_copy(wg_ref, wg_hbm, sems.at[1])]
    for copy in copies:
        copy.start()
    for copy in copies:
        copy.wait()


def per_device(n_dp, n_mp, hidden, qkv, helper, segments, grad_attn):
    width, tokens = qkv.shape[1], qkv.shape[2]
    rows = hidden.shape[0] * n_mp // n_dp
    win = segments.shape[1]
    pair = 2 * win
    parts = parts_of(width)
    heads, pairs, groups, far = width // HEAD_DIM, tokens // pair, n_dp // 2, n_mp // 2
    bf16, f32 = jnp.bfloat16, jnp.float32
    vmem, anywhere = pl.BlockSpec(memory_space=pltpu.VMEM), pl.BlockSpec(memory_space=pltpu.HBM)
    dma = pltpu.SemaphoreType.DMA
    pieces = pieces_of(width)
    bits = groups.bit_length() - 1
    cut = halved(pieces, parts)
    incoming = [[pltpu.VMEM((groups >> (b + 1),) + shape_sent(rows, size), bf16) for b in range(bits)] for _, size in cut]
    kinds = sorted({size for _, size in cut})
    outgoing = [[pltpu.VMEM((sum(size == kind for _, size in cut), groups >> (b + 1)) + shape_sent(rows, kind), bf16)
                 for b in range(bits)] for kind in kinds]
    straight = pltpu.VMEM((max(len(pieces) - len(cut), 1), groups - 1) + shape_sent(rows, pieces[-1][1]), bf16)
    split = hidden.reshape(-1, 2, rows, tokens)
    token_grads, weight_grad = pl.pallas_call(
        functools.partial(kernel, n_dp, n_mp),
        out_shape=(
            pltpu.VMEM((3 * width, tokens), bf16),
            pltpu.VMEM((3, rows, width), f32),
        ),
        in_specs=[anywhere] * 5,
        out_specs=(vmem, vmem),
        scratch_shapes=[
            pltpu.SMEM(helper.shape[:1], jnp.int32),
            pltpu.VMEM(segments.shape, jnp.int32),
            pltpu.VMEM(split.shape, bf16),
            pltpu.VMEM(qkv.shape, bf16),
            pltpu.VMEM(grad_attn.shape, bf16),
            pltpu.VMEM((3 * width, tokens), bf16),
            pltpu.VMEM((n_dp, 1, pair), jnp.int32),
            pltpu.VMEM((n_dp, 1, pair), jnp.int32),
            pltpu.VMEM((parts, n_dp, width // parts // 2, pair), bf16),
            [pltpu.VMEM((n_dp, width // parts // 2, pair), bf16) for _ in range(parts)],
            pltpu.VMEM((2, groups, rows, tokens), bf16),
            pltpu.VMEM((pairs * heads, pair, pair), f32),
            pltpu.VMEM((width, tokens), bf16),
            [pltpu.VMEM((groups, rows, size), f32) for _, size in pieces],
            outgoing,
            incoming,
            straight,
            straight,
            dma((5,)),
            dma, dma, dma((parts,)), dma((parts,)),
            dma, dma((5 if rows % 80 == 0 else 1,)), dma, dma, dma, dma, dma((2,)), dma((2,)), dma,
            dma, dma((len(pieces),)), dma((len(kinds), bits)), dma((len(cut), bits)),
            dma, dma,
        ],
        compiler_params=pltpu.CompilerParams(
            collective_id=0, has_side_effects=True, vmem_limit_bytes=65000000
        ),
    )(helper[:, 0], split, qkv, segments, grad_attn)
    token_grads, weight_grad = pl.pallas_call(
        write_out,
        out_shape=(
            jax.ShapeDtypeStruct(token_grads.shape, bf16),
            jax.ShapeDtypeStruct(weight_grad.shape, f32),
        ),
        in_specs=[vmem, vmem],
        out_specs=(anywhere, anywhere),
        scratch_shapes=[dma((2,))],
        compiler_params=pltpu.CompilerParams(vmem_limit_bytes=8 * 1024 * 1024),
    )(token_grads, weight_grad)
    return token_grads.reshape(qkv.shape), jnp.transpose(weight_grad, (1, 0, 2))


def solution(mesh):
    in_specs = (P("mp", "dp"), P(None, "mp", "dp"), P("dp", None), P("dp", None), P("mp", "dp"))
    out_specs = (P(None, "mp", "dp"), P("dp", None, "mp"))
    return jax.shard_map(
        functools.partial(per_device, mesh.shape["dp"], mesh.shape["mp"]),
        mesh=mesh, in_specs=in_specs, out_specs=out_specs, check_vma=False,
    )
```

```python
import functools
import math

import jax
import jax.numpy as jnp
from jax import lax
from jax.experimental import pallas as pl
from jax.experimental.pallas import tpu as pltpu
from jax.sharding import PartitionSpec as P

HEAD_DIM = 80
DIRECT_PIECES = 1
MESH = pl.DeviceIdType.MESH


def contract(a, b, dims):
    return lax.dot_general(a, b, (dims, ((), ())), preferred_element_type=jnp.float32)


def parts_of(width):
    return 2 if width // HEAD_DIM % 2 == 0 and width >= 256 else 1


def pieces_of(width):
    lanes, parts = 128, parts_of(width)
    if parts == 1:
        sizes = [3 * width % lanes] * (3 * width % lanes > 0) + [lanes] * (3 * width // lanes)
        out, high = [], 3 * width
        for size in sizes:
            high -= size
            out.append((high, size))
        return out
    upper, lower = [], []
    for j in (2, 1, 0):
        high = (j + 1) * width
        for i in range(width // parts // lanes):
            high -= lanes
            upper += [(high + lanes // 2, lanes // 2), (high, lanes // 2)] if j == 2 and i == 0 else [(high, lanes)]
        while high > j * width:
            size = min(lanes, high - j * width)
            high -= size
            lower.append((high, size))
    return upper + lower


def halved(pieces, parts):
    return pieces[:len(pieces) - DIRECT_PIECES] if parts > 1 else pieces


def shape_sent(rows, size):
    return (rows // 2, 2 * size) if 2 * size <= 128 and rows % 32 == 0 else (rows, size)


def kernel(n_dp, n_mp, helper_hbm, hid_hbm, qkv_hbm, seg_hbm, ga_hbm, tg_ref, wg_ref,
           helper_ref, seg_ref, hid_ref, qkv_ref, ga_ref, mate_tg,
           seg_send, seg_recv, ga_send, ga_recv, hid_all, prob_s, dout_s, acc, sends, recvs, straight_out, straight_in,
           load_sem, seg_ss, seg_rs, ga_ss, ga_rs, hx_ss, hx_rs, hz_ss, hz_rs, hy_ss, hy_rs, hp_ss, hp_rs, own_sem,
           tg_ss, tg_rs, st_ss, st_rs, di_ss, di_rs):
    d = lax.axis_index("dp")
    m = lax.axis_index("mp")
    y, c = m // 2, m % 2
    z, x = d // 2, d % 2
    far, groups = n_mp // 2, n_dp // 2
    win = seg_ref.shape[1]
    pair = 2 * win
    width, tokens = qkv_ref.shape[1], qkv_ref.shape[2]
    heads, pairs = width // HEAD_DIM, tokens // pair
    parts = parts_of(width)
    band = width // parts
    half = band // 2
    blocks, rows = hid_ref.shape[0], hid_ref.shape[2]
    scale = 1.0 / math.sqrt(HEAD_DIM)
    mate = 2 * y + 1 - c
    beside = 2 * z + 1 - x
    pieces = pieces_of(width)
    bits = groups.bit_length() - 1
    bf16, f32 = jnp.bfloat16, jnp.float32

    loads = [pltpu.make_async_copy(a, b, load_sem.at[i])
             for i, (a, b) in enumerate(((ga_hbm, ga_ref), (hid_hbm, hid_ref), (qkv_hbm, qkv_ref),
                                         (seg_hbm, seg_ref), (helper_hbm, helper_ref)))]
    for i in (0, 3, 1, 2, 4):
        loads[i].start()

    barrier = pltpu.get_barrier_semaphore()
    for k in range(1, n_dp):
        pl.semaphore_signal(barrier, inc=1, device_id={"dp": lax.rem(d + k, n_dp)}, device_id_type=MESH)
    for k in range(1, far):
        pl.semaphore_signal(barrier, inc=1, device_id={"mp": 2 * lax.rem(y + k, far) + c}, device_id_type=MESH)
    pl.semaphore_signal(barrier, inc=1, device_id={"mp": mate}, device_id_type=MESH)

    loads[0].wait()
    lane = lax.broadcasted_iota(jnp.int32, (half, pair), 1)
    low = lane < win
    for j in range(n_dp // 2):
        both = ga_ref[:, j * pair:(j + 1) * pair].astype(f32)
        for g in range(parts):
            top, bottom = both[g * band:g * band + half], both[g * band + half:(g + 1) * band]
            ga_send[g, 2 * j] = jnp.where(low, top, pltpu.roll(bottom, win, 1)).astype(bf16)
            ga_send[g, 2 * j + 1] = jnp.where(low, pltpu.roll(top, win, 1), bottom).astype(bf16)
    for g in range(parts):
        ga_recv[g][d] = ga_send[g, d]
    loads[3].wait()
    seg = seg_ref[...]
    seg_twice = jnp.concatenate([seg, seg], axis=1)
    for o in range(n_dp):
        seg_send[o] = seg_twice[o:o + 1]
    seg_recv[d] = seg_send[d]
    loads[1].wait()

    def seg_copy(k):
        to = lax.rem(d + k, n_dp)
        return pltpu.make_async_remote_copy(seg_send.at[to], seg_recv.at[d], seg_ss, seg_rs,
                                            device_id={"dp": to}, device_id_type=MESH)

    others = pl.ds(0, n_dp - 1)
    seg_all = pltpu.make_async_remote_copy(seg_send.at[others], seg_recv.at[others], seg_ss, seg_rs,
                                           device_id={"dp": beside}, device_id_type=MESH)

    def ga_copy(g, k):
        to = lax.rem(d + k, n_dp)
        return pltpu.make_async_remote_copy(ga_send.at[g, to], ga_recv[g].at[d], ga_ss.at[g], ga_rs.at[g],
                                            device_id={"dp": to}, device_id_type=MESH)

    def ga_all(g):
        return pltpu.make_async_remote_copy(ga_send.at[g, others], ga_recv[g].at[others], ga_ss.at[g], ga_rs.at[g],
                                            device_id={"dp": beside}, device_id_type=MESH)

    def hid_at(side, member):
        return hid_all.at[side, pl.ds(member * blocks, blocks)]

    own = pltpu.make_async_copy(hid_ref.at[:, x], hid_at(0, m), own_sem)
    chunks = 5 if rows % 80 == 0 else 1

    def hid_x(q):
        at = pl.ds(q * (rows // chunks), rows // chunks)
        return pltpu.make_async_remote_copy(hid_ref.at[:, 1 - x, at], hid_at(1, m).at[:, at], hx_ss, hx_rs.at[q],
                                            device_id={"dp": beside}, device_id_type=MESH)

    def pass_copy(q, k):
        at = pl.ds(q * (rows // chunks), rows // chunks)
        return pltpu.make_async_remote_copy(hid_at(1, m).at[:, at], hid_at(1, m).at[:, at], hz_ss, hz_rs,
                                            device_id={"mp": 2 * lax.rem(y + k, far) + c}, device_id_type=MESH)

    def hid_copy(k):
        return pltpu.make_async_remote_copy(hid_ref.at[:, x], hid_at(0, m), hy_ss, hy_rs,
                                            device_id={"mp": 2 * lax.rem(y + k, far) + c}, device_id_type=MESH)

    def mate_copy(side, k):
        at = hid_at(side, 2 * lax.rem(y - k + far, far) + c)
        src = hid_ref.at[:, x] if (side, k) == (0, 0) else at
        return pltpu.make_async_remote_copy(src, at, hp_ss.at[side], hp_rs.at[side],
                                            device_id={"mp": mate}, device_id_type=MESH)

    def members(side, count, send, recv):
        at = hid_all.at[side, pl.ds(0, count * blocks)]
        return pltpu.make_async_remote_copy(at, at, send, recv, device_id={"mp": mate}, device_id_type=MESH)

    pl.semaphore_wait(barrier, n_dp - 1 + far)
    for k in range(1, n_dp):
        seg_copy(k).start()
    for k in range(1, far):
        hid_copy(k).start()
    for k in range(1, n_dp):
        ga_copy(parts - 1, k).start()
    for q in range(chunks):
        hid_x(q).start()
    mate_copy(0, 0).start()
    own.start()
    loads[2].wait()
    loads[4].wait()

    def at_of(p, h):
        return slice(h * HEAD_DIM, (h + 1) * HEAD_DIM), slice(p * pair, (p + 1) * pair)

    for p in range(pairs):
        for h in range(heads):
            at = at_of(p, h)
            prob_s[p * heads + h] = contract(qkv_ref[(1,) + at], qkv_ref[(0,) + at], ((0,), (0,))) * scale
    seg_all.wait()
    lane_row = lax.broadcasted_iota(jnp.int32, (1, pair), 1)
    for p in range(pairs):
        first, second = seg_recv[helper_ref[2 * p]], seg_recv[helper_ref[2 * p + 1]]
        name = jnp.where(lane_row < win, first, second + 2).astype(f32)
        across = jnp.broadcast_to(name, (pair, pair))
        same = across == across.T
        for h in range(heads):
            scores = jnp.where(same, prob_s[p * heads + h], -1e30)
            prob = jnp.exp(scores - jnp.max(scores, axis=0, keepdims=True))
            prob_s[p * heads + h] = prob / jnp.sum(prob, axis=0, keepdims=True)

    def pass_on(q):
        hid_x(q).wait_recv()
        for k in range(1, far):
            pass_copy(q, k).start()

    before = min(2, chunks)
    for q in range(before):
        pass_on(q)
    for g in range(parts - 1):
        for k in range(1, n_dp):
            ga_copy(g, k).start()

    def tg_copy(s):
        at = pl.ds(*pieces[s])
        return pltpu.make_async_remote_copy(tg_ref.at[at], mate_tg.at[at], tg_ss, tg_rs.at[s],
                                            device_id={"dp": beside}, device_id_type=MESH)

    def put(j, p, h, grads):
        tg_ref[j * width + h * HEAD_DIM:j * width + (h + 1) * HEAD_DIM, p * pair:(p + 1) * pair] = grads.astype(bf16)

    def dv(g, p):
        first = ga_recv[g][helper_ref[2 * p]].astype(f32)
        second = ga_recv[g][helper_ref[2 * p + 1]].astype(f32)
        top = jnp.where(low, first, pltpu.roll(second, win, 1))
        bottom = jnp.where(low, pltpu.roll(first, win, 1), second)
        dout_s[g * band:(g + 1) * band, p * pair:(p + 1) * pair] = jnp.concatenate([top, bottom], axis=0).astype(bf16)
        for h in range(g * heads // parts, (g + 1) * heads // parts):
            put(2, p, h, contract(dout_s[at_of(p, h)], prob_s[p * heads + h].astype(bf16), ((1,), (1,))))

    def attend(g, p):
        for h in range(g * heads // parts, (g + 1) * heads // parts):
            at = at_of(p, h)
            query, key, value = qkv_ref[(0,) + at], qkv_ref[(1,) + at], qkv_ref[(2,) + at]
            prob = prob_s[p * heads + h]
            dprob = contract(value, dout_s[at], ((0,), (0,)))
            delta = jnp.sum(prob.astype(bf16).astype(f32) * dprob, axis=0, keepdims=True)
            dscore = (prob * (dprob - delta)).astype(bf16)
            put(0, p, h, contract(key, dscore, ((1,), (0,))) * scale)
            put(1, p, h, contract(query, dscore, ((1,), (1,))) * scale)

    sent = []

    def send_ready(g, j):
        for s, (start, size) in enumerate(pieces):
            if s not in sent and start // width >= j and (start % width >= g * band or parts == 1 or g == 0):
                if start // width == 2 or j < 2:
                    tg_copy(s).start()
                    sent.append(s)

    later = max(before, chunks - 1)
    for g in reversed(range(parts)):
        ga_all(g).wait()
        for p in range(pairs):
            dv(g, p)
        send_ready(g, 2)
        if g == parts - 1:
            for q in range(before, later):
                pass_on(q)
            members(0, far - 1, hy_ss, hy_rs).wait()
            for k in range(1, far):
                mate_copy(0, k).start()
        for p in range(pairs if g > 0 else 0):
            if p == 1:
                for q in range(later, chunks):
                    pass_on(q)
                mate_copy(1, 0).start()
            attend(g, p)
        if g > 0:
            send_ready(g, 0)
    if parts == 1:
        mate_copy(1, 0).start()
    members(1, far - 1, hz_ss, hz_rs).wait()
    for k in range(1, far):
        mate_copy(1, k).start()
    own.wait()
    members(0, far, hp_ss.at[0], hp_rs.at[0]).wait()

    def products(side, of, s, blocks):
        at = slice(pieces[s][0], pieces[s][0] + pieces[s][1])
        if rows % 16 == 0:
            stacked = jnp.concatenate([hid_all[side, t] for t in blocks], axis=0)
            return contract(stacked, of[at], ((1,), (1,))).reshape(len(blocks), rows, pieces[s][1])
        return [contract(hid_all[side, t], of[at], ((1,), (1,))) for t in blocks]

    def mine(s):
        for t, block in enumerate(products(0, tg_ref, s, range(groups))):
            acc[s][t] = block

    def theirs(s, blocks):
        for t, block in zip(blocks, products(1, mate_tg, s, blocks)):
            acc[s][t] = acc[s][t] + block

    def packed(block):
        if block.shape[1] * 2 <= 128 and rows % 32 == 0:
            block = jnp.concatenate([block[:rows // 2], block[rows // 2:]], axis=1)
        return block.astype(bf16)

    def unpacked(block, size):
        block = block.astype(f32)
        if block.shape[1] != size:
            block = jnp.concatenate([block[:, :size], block[:, size:]], axis=0)
        return block

    def finish(s, total):
        start, size = pieces[s]
        for j in range(3):
            a, b = max(start, j * width), min(start + size, (j + 1) * width)
            if a < b:
                wg_ref[j, :, a - j * width:b - j * width] = total[:, a - start:b - start]

    count = len(pieces)
    straight = len(halved(pieces, parts))
    kinds = sorted({size for _, size in pieces[:straight]})
    place = [(kinds.index(size), sum(other == size for _, other in pieces[:s])) for s, (_, size) in enumerate(pieces[:straight])]

    def outgoing(s, b):
        kind, at = place[s]
        return sends[kind][b].at[at]

    def half_copy(s, b):
        bit = z // 2 ** b % 2
        to = z + (1 - 2 * bit) * 2 ** b
        return pltpu.make_async_remote_copy(outgoing(s, b), recvs[s][b], st_ss.at[place[s][0], b], st_rs.at[s, b],
                                            device_id={"dp": 2 * to + x}, device_id_type=MESH)

    def begin(s, b):
        bit = z // 2 ** b % 2
        for i in range(groups >> (b + 1)):
            t = z % 2 ** b + (1 - bit) * 2 ** b + i * 2 ** (b + 1)
            outgoing(s, b)[i] = packed(acc[s][t])
        half_copy(s, b).start()

    def end(s, b):
        half_copy(s, b).wait_recv()
        bit = z // 2 ** b % 2
        for i in range(groups >> (b + 1)):
            t = z % 2 ** b + bit * 2 ** b + i * 2 ** (b + 1)
            acc[s][t] = acc[s][t] + unpacked(recvs[s][b][i], pieces[s][1])

    def direct_copy(s, k):
        return pltpu.make_async_remote_copy(straight_out.at[s, k - 1], straight_in.at[s, k - 1], di_ss, di_rs,
                                            device_id={"dp": 2 * lax.rem(z + k, groups) + x}, device_id_type=MESH)

    def advance(s, b):
        if 0 <= s < straight:
            end(s, b)
            if b + 1 < bits:
                begin(s, b + 1)
            else:
                finish(s, acc[s][z])

    swapped = groups == 4
    inner = z == 2
    ahead = 2 if parts > 1 else 0
    attends = {3: range(pairs // 2), 4: range(pairs // 2, pairs)} if parts > 1 else {0: range(pairs)}
    for s in range(ahead):
        mine(s)
    members(1, far, hp_ss.at[1], hp_rs.at[1]).wait()
    bit = z % 2
    sent_first = [1 - bit + 2 * i for i in range(groups // 2)]
    kept = [bit + 2 * i for i in range(groups // 2)]
    for turn in range(count + 2 + 4 * (bits - 1)):
        for p in attends.get(turn, ()):
            attend(0, p)
        if turn == max(attends):
            send_ready(0, 0)
        if turn < count:
            if turn >= ahead:
                mine(turn)
            tg_copy(turn).wait_recv()
            if turn < straight:
                theirs(turn, sent_first)
                if swapped:
                    pl.when(inner)(functools.partial(advance, turn - 2, 0))
                begin(turn, 0)
                theirs(turn, kept)
            else:
                theirs(turn, range(groups))
                for i in range(groups - 1):
                    t = i + (i >= z).astype(jnp.int32)
                    k = lax.rem(t - z + groups, groups)
                    straight_out[turn - straight, k - 1] = packed(acc[turn][t])
                    direct_copy(turn - straight, k).start()
        for b in range(bits):
            step = functools.partial(advance, turn - 2 - 3 * b, b)
            if swapped and b == 0 and turn < straight:
                pl.when(jnp.logical_not(inner))(step)
            else:
                step()
    if straight < count:
        pltpu.make_async_remote_copy(straight_out, straight_in, di_ss, di_rs,
                                     device_id={"dp": beside}, device_id_type=MESH).wait()
    for s in range(straight, count):
        total = acc[s][z]
        for k in range(1, groups):
            total = total + unpacked(straight_in[s - straight, k - 1], pieces[s][1])
        finish(s, total)
    pltpu.make_async_remote_copy(tg_ref, mate_tg, tg_ss, tg_rs.at[0],
                                 device_id={"dp": beside}, device_id_type=MESH).wait_send()
    pltpu.make_async_remote_copy(hid_ref.at[:, 1 - x], hid_at(1, m), hx_ss, hx_rs.at[0],
                                 device_id={"dp": beside}, device_id_type=MESH).wait_send()
    for kind in range(len(kinds)):
        for b in range(bits):
            pltpu.make_async_remote_copy(sends[kind][b], sends[kind][b], st_ss.at[kind, b], st_rs.at[0, b],
                                         device_id={"dp": beside}, device_id_type=MESH).wait_send()


def write_out(tg_ref, wg_ref, tg_hbm, wg_hbm, sems):
    copies = [pltpu.make_async_copy(tg_ref, tg_hbm, sems.at[0]), pltpu.make_async_copy(wg_ref, wg_hbm, sems.at[1])]
    for copy in copies:
        copy.start()
    for copy in copies:
        copy.wait()


def per_device(n_dp, n_mp, hidden, qkv, helper, segments, grad_attn):
    width, tokens = qkv.shape[1], qkv.shape[2]
    rows = hidden.shape[0] * n_mp // n_dp
    win = segments.shape[1]
    pair = 2 * win
    parts = parts_of(width)
    heads, pairs, groups, far = width // HEAD_DIM, tokens // pair, n_dp // 2, n_mp // 2
    bf16, f32 = jnp.bfloat16, jnp.float32
    vmem, anywhere = pl.BlockSpec(memory_space=pltpu.VMEM), pl.BlockSpec(memory_space=pltpu.HBM)
    dma = pltpu.SemaphoreType.DMA
    pieces = pieces_of(width)
    bits = groups.bit_length() - 1
    cut = halved(pieces, parts)
    incoming = [[pltpu.VMEM((groups >> (b + 1),) + shape_sent(rows, size), bf16) for b in range(bits)] for _, size in cut]
    kinds = sorted({size for _, size in cut})
    outgoing = [[pltpu.VMEM((sum(size == kind for _, size in cut), groups >> (b + 1)) + shape_sent(rows, kind), bf16)
                 for b in range(bits)] for kind in kinds]
    straight = pltpu.VMEM((max(len(pieces) - len(cut), 1), groups - 1) + shape_sent(rows, pieces[-1][1]), bf16)
    split = hidden.reshape(-1, 2, rows, tokens)
    token_grads, weight_grad = pl.pallas_call(
        functools.partial(kernel, n_dp, n_mp),
        out_shape=(
            pltpu.VMEM((3 * width, tokens), bf16),
            pltpu.VMEM((3, rows, width), f32),
        ),
        in_specs=[anywhere] * 5,
        out_specs=(vmem, vmem),
        scratch_shapes=[
            pltpu.SMEM(helper.shape[:1], jnp.int32),
            pltpu.VMEM(segments.shape, jnp.int32),
            pltpu.VMEM(split.shape, bf16),
            pltpu.VMEM(qkv.shape, bf16),
            pltpu.VMEM(grad_attn.shape, bf16),
            pltpu.VMEM((3 * width, tokens), bf16),
            pltpu.VMEM((n_dp, 1, pair), jnp.int32),
            pltpu.VMEM((n_dp, 1, pair), jnp.int32),
            pltpu.VMEM((parts, n_dp, width // parts // 2, pair), bf16),
            [pltpu.VMEM((n_dp, width // parts // 2, pair), bf16) for _ in range(parts)],
            pltpu.VMEM((2, groups, rows, tokens), bf16),
            pltpu.VMEM((pairs * heads, pair, pair), f32),
            pltpu.VMEM((width, tokens), bf16),
            [pltpu.VMEM((groups, rows, size), f32) for _, size in pieces],
            outgoing,
            incoming,
            straight,
            straight,
            dma((5,)),
            dma, dma, dma((parts,)), dma((parts,)),
            dma, dma((5 if rows % 80 == 0 else 1,)), dma, dma, dma, dma, dma((2,)), dma((2,)), dma,
            dma, dma((len(pieces),)), dma((len(kinds), bits)), dma((len(cut), bits)),
            dma, dma,
        ],
        compiler_params=pltpu.CompilerParams(
            collective_id=0, has_side_effects=True, vmem_limit_bytes=65000000
        ),
    )(helper[:, 0], split, qkv, segments, grad_attn)
    token_grads, weight_grad = pl.pallas_call(
        write_out,
        out_shape=(
            jax.ShapeDtypeStruct(token_grads.shape, bf16),
            jax.ShapeDtypeStruct(weight_grad.shape, f32),
        ),
        in_specs=[vmem, vmem],
        out_specs=(anywhere, anywhere),
        scratch_shapes=[dma((2,))],
        compiler_params=pltpu.CompilerParams(vmem_limit_bytes=8 * 1024 * 1024),
    )(token_grads, weight_grad)
    return token_grads.reshape(qkv.shape), jnp.transpose(weight_grad, (1, 0, 2))


def solution(mesh):
    in_specs = (P("mp", "dp"), P(None, "mp", "dp"), P("dp", None), P("dp", None), P("mp", "dp"))
    out_specs = (P(None, "mp", "dp"), P("dp", None, "mp"))
    return jax.shard_map(
        functools.partial(per_device, mesh.shape["dp"], mesh.shape["mp"]),
        mesh=mesh, in_specs=in_specs, out_specs=out_specs, check_vma=False,
    )
```

```python
import functools
import math

import jax
import jax.numpy as jnp
from jax import lax
from jax.experimental import pallas as pl
from jax.experimental.pallas import tpu as pltpu
from jax.sharding import PartitionSpec as P

HEAD_DIM = 80
DIRECT_PIECES = 1
MESH = pl.DeviceIdType.MESH


def contract(a, b, dims):
    return lax.dot_general(a, b, (dims, ((), ())), preferred_element_type=jnp.float32)


def parts_of(width):
    return 2 if width // HEAD_DIM % 2 == 0 and width >= 256 else 1


def pieces_of(width):
    lanes, parts = 128, parts_of(width)
    if parts == 1:
        sizes = [3 * width % lanes] * (3 * width % lanes > 0) + [lanes] * (3 * width // lanes)
        out, high = [], 3 * width
        for size in sizes:
            high -= size
            out.append((high, size))
        return out
    upper, lower = [], []
    for j in (2, 1, 0):
        high = (j + 1) * width
        for i in range(width // parts // lanes):
            high -= lanes
            upper += [(high + lanes // 2, lanes // 2), (high, lanes // 2)] if j == 2 and i == 0 else [(high, lanes)]
        while high > j * width:
            size = min(lanes, high - j * width)
            high -= size
            lower.append((high, size))
    return upper + lower


def halved(pieces, parts):
    return pieces[:len(pieces) - DIRECT_PIECES] if parts > 1 else pieces


def shape_sent(rows, size):
    return (rows // 2, 2 * size) if 2 * size <= 128 and rows % 32 == 0 else (rows, size)


def kernel(n_dp, n_mp, helper_hbm, hid_hbm, qkv_hbm, seg_hbm, ga_hbm, tg_ref, wg_ref,
           helper_ref, seg_ref, hid_ref, qkv_ref, ga_ref, mate_tg,
           seg_send, seg_recv, ga_send, ga_recv, hid_all, prob_s, dout_s, acc, sends, recvs, straight_out, straight_in,
           load_sem, seg_ss, seg_rs, ga_ss, ga_rs, hx_ss, hx_rs, hz_ss, hz_rs, hy_ss, hy_rs, hp_ss, hp_rs, own_sem,
           tg_ss, tg_rs, st_ss, st_rs, di_ss, di_rs):
    d = lax.axis_index("dp")
    m = lax.axis_index("mp")
    y, c = m // 2, m % 2
    z, x = d // 2, d % 2
    far, groups = n_mp // 2, n_dp // 2
    win = seg_ref.shape[1]
    pair = 2 * win
    width, tokens = qkv_ref.shape[1], qkv_ref.shape[2]
    heads, pairs = width // HEAD_DIM, tokens // pair
    parts = parts_of(width)
    band = width // parts
    half = band // 2
    blocks, rows = hid_ref.shape[0], hid_ref.shape[2]
    scale = 1.0 / math.sqrt(HEAD_DIM)
    mate = 2 * y + 1 - c
    beside = 2 * z + 1 - x
    pieces = pieces_of(width)
    bits = groups.bit_length() - 1
    bf16, f32 = jnp.bfloat16, jnp.float32

    loads = [pltpu.make_async_copy(a, b, load_sem.at[i])
             for i, (a, b) in enumerate(((ga_hbm, ga_ref), (hid_hbm, hid_ref), (qkv_hbm, qkv_ref),
                                         (seg_hbm, seg_ref), (helper_hbm, helper_ref)))]
    for i in (0, 3, 1, 2, 4):
        loads[i].start()

    barrier = pltpu.get_barrier_semaphore()
    for k in range(1, n_dp):
        pl.semaphore_signal(barrier, inc=1, device_id={"dp": lax.rem(d + k, n_dp)}, device_id_type=MESH)
    for k in range(1, far):
        pl.semaphore_signal(barrier, inc=1, device_id={"mp": 2 * lax.rem(y + k, far) + c}, device_id_type=MESH)
    pl.semaphore_signal(barrier, inc=1, device_id={"mp": mate}, device_id_type=MESH)

    loads[0].wait()
    lane = lax.broadcasted_iota(jnp.int32, (half, pair), 1)
    low = lane < win
    for j in range(n_dp // 2):
        both = ga_ref[:, j * pair:(j + 1) * pair].astype(f32)
        for g in range(parts):
            top, bottom = both[g * band:g * band + half], both[g * band + half:(g + 1) * band]
            ga_send[g, 2 * j] = jnp.where(low, top, pltpu.roll(bottom, win, 1)).astype(bf16)
            ga_send[g, 2 * j + 1] = jnp.where(low, pltpu.roll(top, win, 1), bottom).astype(bf16)
    for g in range(parts):
        ga_recv[g][d] = ga_send[g, d]
    loads[3].wait()
    seg = seg_ref[...]
    seg_twice = jnp.concatenate([seg, seg], axis=1)
    for o in range(n_dp):
        seg_send[o] = seg_twice[o:o + 1]
    seg_recv[d] = seg_send[d]
    loads[1].wait()

    def seg_copy(k):
        to = lax.rem(d + k, n_dp)
        return pltpu.make_async_remote_copy(seg_send.at[to], seg_recv.at[d], seg_ss, seg_rs,
                                            device_id={"dp": to}, device_id_type=MESH)

    others = pl.ds(0, n_dp - 1)
    seg_all = pltpu.make_async_remote_copy(seg_send.at[others], seg_recv.at[others], seg_ss, seg_rs,
                                           device_id={"dp": beside}, device_id_type=MESH)

    def ga_copy(g, k):
        to = lax.rem(d + k, n_dp)
        return pltpu.make_async_remote_copy(ga_send.at[g, to], ga_recv[g].at[d], ga_ss.at[g], ga_rs.at[g],
                                            device_id={"dp": to}, device_id_type=MESH)

    def ga_all(g):
        return pltpu.make_async_remote_copy(ga_send.at[g, others], ga_recv[g].at[others], ga_ss.at[g], ga_rs.at[g],
                                            device_id={"dp": beside}, device_id_type=MESH)

    def hid_at(side, member):
        return hid_all.at[side, pl.ds(member * blocks, blocks)]

    own = pltpu.make_async_copy(hid_ref.at[:, x], hid_at(0, m), own_sem)
    chunks = 5 if rows % 80 == 0 else 1

    def hid_x(q):
        at = pl.ds(q * (rows // chunks), rows // chunks)
        return pltpu.make_async_remote_copy(hid_ref.at[:, 1 - x, at], hid_at(1, m).at[:, at], hx_ss, hx_rs.at[q],
                                            device_id={"dp": beside}, device_id_type=MESH)

    def pass_copy(q, k):
        at = pl.ds(q * (rows // chunks), rows // chunks)
        return pltpu.make_async_remote_copy(hid_at(1, m).at[:, at], hid_at(1, m).at[:, at], hz_ss, hz_rs,
                                            device_id={"mp": 2 * lax.rem(y + k, far) + c}, device_id_type=MESH)

    def hid_copy(k):
        return pltpu.make_async_remote_copy(hid_ref.at[:, x], hid_at(0, m), hy_ss, hy_rs,
                                            device_id={"mp": 2 * lax.rem(y + k, far) + c}, device_id_type=MESH)

    def mate_copy(side, k):
        at = hid_at(side, 2 * lax.rem(y - k + far, far) + c)
        src = hid_ref.at[:, x] if (side, k) == (0, 0) else at
        return pltpu.make_async_remote_copy(src, at, hp_ss.at[side], hp_rs.at[side],
                                            device_id={"mp": mate}, device_id_type=MESH)

    def members(side, count, send, recv):
        at = hid_all.at[side, pl.ds(0, count * blocks)]
        return pltpu.make_async_remote_copy(at, at, send, recv, device_id={"mp": mate}, device_id_type=MESH)

    pl.semaphore_wait(barrier, n_dp - 1 + far)
    for k in range(1, n_dp):
        seg_copy(k).start()
    for k in range(1, far):
        hid_copy(k).start()
    for k in (*range(1, n_dp, 2), *range(2, n_dp, 2)):
        ga_copy(parts - 1, k).start()
    for q in range(chunks):
        hid_x(q).start()
    mate_copy(0, 0).start()
    own.start()
    loads[2].wait()
    loads[4].wait()

    def at_of(p, h):
        return slice(h * HEAD_DIM, (h + 1) * HEAD_DIM), slice(p * pair, (p + 1) * pair)

    for p in range(pairs):
        for h in range(heads):
            at = at_of(p, h)
            prob_s[p * heads + h] = contract(qkv_ref[(1,) + at], qkv_ref[(0,) + at], ((0,), (0,))) * scale
    seg_all.wait()
    lane_row = lax.broadcasted_iota(jnp.int32, (1, pair), 1)
    for p in range(pairs):
        first, second = seg_recv[helper_ref[2 * p]], seg_recv[helper_ref[2 * p + 1]]
        name = jnp.where(lane_row < win, first, second + 2).astype(f32)
        across = jnp.broadcast_to(name, (pair, pair))
        same = across == across.T
        for h in range(heads):
            scores = jnp.where(same, prob_s[p * heads + h], -1e30)
            prob = jnp.exp(scores - jnp.max(scores, axis=0, keepdims=True))
            prob_s[p * heads + h] = prob / jnp.sum(prob, axis=0, keepdims=True)

    def pass_on(q):
        hid_x(q).wait_recv()
        for k in range(1, far):
            pass_copy(q, k).start()

    before = min(2, chunks)
    for q in range(before):
        pass_on(q)
    for g in range(parts - 1):
        for k in range(1, n_dp):
            ga_copy(g, k).start()

    def tg_copy(s):
        at = pl.ds(*pieces[s])
        return pltpu.make_async_remote_copy(tg_ref.at[at], mate_tg.at[at], tg_ss, tg_rs.at[s],
                                            device_id={"dp": beside}, device_id_type=MESH)

    def put(j, p, h, grads):
        tg_ref[j * width + h * HEAD_DIM:j * width + (h + 1) * HEAD_DIM, p * pair:(p + 1) * pair] = grads.astype(bf16)

    def dv(g, p):
        first = ga_recv[g][helper_ref[2 * p]].astype(f32)
        second = ga_recv[g][helper_ref[2 * p + 1]].astype(f32)
        top = jnp.where(low, first, pltpu.roll(second, win, 1))
        bottom = jnp.where(low, pltpu.roll(first, win, 1), second)
        dout_s[g * band:(g + 1) * band, p * pair:(p + 1) * pair] = jnp.concatenate([top, bottom], axis=0).astype(bf16)
        for h in range(g * heads // parts, (g + 1) * heads // parts):
            put(2, p, h, contract(dout_s[at_of(p, h)], prob_s[p * heads + h].astype(bf16), ((1,), (1,))))

    def attend(g, p):
        for h in range(g * heads // parts, (g + 1) * heads // parts):
            at = at_of(p, h)
            query, key, value = qkv_ref[(0,) + at], qkv_ref[(1,) + at], qkv_ref[(2,) + at]
            prob = prob_s[p * heads + h]
            dprob = contract(value, dout_s[at], ((0,), (0,)))
            delta = jnp.sum(prob.astype(bf16).astype(f32) * dprob, axis=0, keepdims=True)
            dscore = (prob * (dprob - delta)).astype(bf16)
            put(0, p, h, contract(key, dscore, ((1,), (0,))) * scale)
            put(1, p, h, contract(query, dscore, ((1,), (1,))) * scale)

    sent = []

    def send_ready(g, j):
        for s, (start, size) in enumerate(pieces):
            if s not in sent and start // width >= j and (start % width >= g * band or parts == 1 or g == 0):
                if start // width == 2 or j < 2:
                    tg_copy(s).start()
                    sent.append(s)

    later = max(before, chunks - 1)
    for g in reversed(range(parts)):
        ga_all(g).wait()
        for p in range(pairs):
            dv(g, p)
        send_ready(g, 2)
        if g == parts - 1:
            for q in range(before, later):
                pass_on(q)
            members(0, far - 1, hy_ss, hy_rs).wait()
            for k in range(1, far):
                mate_copy(0, k).start()
        for p in range(pairs if g > 0 else 0):
            if p == 1:
                for q in range(later, chunks):
                    pass_on(q)
                mate_copy(1, 0).start()
            attend(g, p)
        if g > 0:
            send_ready(g, 0)
    if parts == 1:
        mate_copy(1, 0).start()
    members(1, far - 1, hz_ss, hz_rs).wait()
    for k in range(1, far):
        mate_copy(1, k).start()
    own.wait()
    members(0, far, hp_ss.at[0], hp_rs.at[0]).wait()

    def products(side, of, s, blocks):
        at = slice(pieces[s][0], pieces[s][0] + pieces[s][1])
        if rows % 16 == 0:
            stacked = jnp.concatenate([hid_all[side, t] for t in blocks], axis=0)
            return contract(stacked, of[at], ((1,), (1,))).reshape(len(blocks), rows, pieces[s][1])
        return [contract(hid_all[side, t], of[at], ((1,), (1,))) for t in blocks]

    def mine(s):
        for t, block in enumerate(products(0, tg_ref, s, range(groups))):
            acc[s][t] = block

    def theirs(s, blocks):
        for t, block in zip(blocks, products(1, mate_tg, s, blocks)):
            acc[s][t] = acc[s][t] + block

    def packed(block):
        if block.shape[1] * 2 <= 128 and rows % 32 == 0:
            block = jnp.concatenate([block[:rows // 2], block[rows // 2:]], axis=1)
        return block.astype(bf16)

    def unpacked(block, size):
        block = block.astype(f32)
        if block.shape[1] != size:
            block = jnp.concatenate([block[:, :size], block[:, size:]], axis=0)
        return block

    def finish(s, total):
        start, size = pieces[s]
        for j in range(3):
            a, b = max(start, j * width), min(start + size, (j + 1) * width)
            if a < b:
                wg_ref[j, :, a - j * width:b - j * width] = total[:, a - start:b - start]

    count = len(pieces)
    straight = len(halved(pieces, parts))
    kinds = sorted({size for _, size in pieces[:straight]})
    place = [(kinds.index(size), sum(other == size for _, other in pieces[:s])) for s, (_, size) in enumerate(pieces[:straight])]

    def outgoing(s, b):
        kind, at = place[s]
        return sends[kind][b].at[at]

    def half_copy(s, b):
        bit = z // 2 ** b % 2
        to = z + (1 - 2 * bit) * 2 ** b
        return pltpu.make_async_remote_copy(outgoing(s, b), recvs[s][b], st_ss.at[place[s][0], b], st_rs.at[s, b],
                                            device_id={"dp": 2 * to + x}, device_id_type=MESH)

    def begin(s, b):
        bit = z // 2 ** b % 2
        for i in range(groups >> (b + 1)):
            t = z % 2 ** b + (1 - bit) * 2 ** b + i * 2 ** (b + 1)
            outgoing(s, b)[i] = packed(acc[s][t])
        half_copy(s, b).start()

    def end(s, b):
        half_copy(s, b).wait_recv()
        bit = z // 2 ** b % 2
        for i in range(groups >> (b + 1)):
            t = z % 2 ** b + bit * 2 ** b + i * 2 ** (b + 1)
            acc[s][t] = acc[s][t] + unpacked(recvs[s][b][i], pieces[s][1])

    def direct_copy(s, k):
        return pltpu.make_async_remote_copy(straight_out.at[s, k - 1], straight_in.at[s, k - 1], di_ss, di_rs,
                                            device_id={"dp": 2 * lax.rem(z + k, groups) + x}, device_id_type=MESH)

    def advance(s, b):
        if 0 <= s < straight:
            end(s, b)
            if b + 1 < bits:
                begin(s, b + 1)
            else:
                finish(s, acc[s][z])

    swapped = groups == 4
    inner = z == 2
    ahead = 2 if parts > 1 else 0
    attends = {3: range(pairs // 2), 4: range(pairs // 2, pairs)} if parts > 1 else {0: range(pairs)}
    for s in range(ahead):
        mine(s)
    members(1, far, hp_ss.at[1], hp_rs.at[1]).wait()
    bit = z % 2
    sent_first = [1 - bit + 2 * i for i in range(groups // 2)]
    kept = [bit + 2 * i for i in range(groups // 2)]
    for turn in range(count + 2 + 4 * (bits - 1)):
        for p in attends.get(turn, ()):
            attend(0, p)
        if turn == max(attends):
            send_ready(0, 0)
        if turn < count:
            if turn >= ahead:
                mine(turn)
            tg_copy(turn).wait_recv()
            if turn < straight:
                theirs(turn, sent_first)
                if swapped:
                    pl.when(inner)(functools.partial(advance, turn - 2, 0))
                begin(turn, 0)
                theirs(turn, kept)
            else:
                theirs(turn, range(groups))
                for i in range(groups - 1):
                    t = i + (i >= z).astype(jnp.int32)
                    k = lax.rem(t - z + groups, groups)
                    straight_out[turn - straight, k - 1] = packed(acc[turn][t])
                    direct_copy(turn - straight, k).start()
        for b in range(bits):
            step = functools.partial(advance, turn - 2 - 3 * b, b)
            if swapped and b == 0 and turn < straight:
                pl.when(jnp.logical_not(inner))(step)
            else:
                step()
    if straight < count:
        pltpu.make_async_remote_copy(straight_out, straight_in, di_ss, di_rs,
                                     device_id={"dp": beside}, device_id_type=MESH).wait()
    for s in range(straight, count):
        total = acc[s][z]
        for k in range(1, groups):
            total = total + unpacked(straight_in[s - straight, k - 1], pieces[s][1])
        finish(s, total)
    pltpu.make_async_remote_copy(tg_ref, mate_tg, tg_ss, tg_rs.at[0],
                                 device_id={"dp": beside}, device_id_type=MESH).wait_send()
    pltpu.make_async_remote_copy(hid_ref.at[:, 1 - x], hid_at(1, m), hx_ss, hx_rs.at[0],
                                 device_id={"dp": beside}, device_id_type=MESH).wait_send()
    for kind in range(len(kinds)):
        for b in range(bits):
            pltpu.make_async_remote_copy(sends[kind][b], sends[kind][b], st_ss.at[kind, b], st_rs.at[0, b],
                                         device_id={"dp": beside}, device_id_type=MESH).wait_send()


def write_out(tg_ref, wg_ref, tg_hbm, wg_hbm, sems):
    copies = [pltpu.make_async_copy(tg_ref, tg_hbm, sems.at[0]), pltpu.make_async_copy(wg_ref, wg_hbm, sems.at[1])]
    for copy in copies:
        copy.start()
    for copy in copies:
        copy.wait()


def per_device(n_dp, n_mp, hidden, qkv, helper, segments, grad_attn):
    width, tokens = qkv.shape[1], qkv.shape[2]
    rows = hidden.shape[0] * n_mp // n_dp
    win = segments.shape[1]
    pair = 2 * win
    parts = parts_of(width)
    heads, pairs, groups, far = width // HEAD_DIM, tokens // pair, n_dp // 2, n_mp // 2
    bf16, f32 = jnp.bfloat16, jnp.float32
    vmem, anywhere = pl.BlockSpec(memory_space=pltpu.VMEM), pl.BlockSpec(memory_space=pltpu.HBM)
    dma = pltpu.SemaphoreType.DMA
    pieces = pieces_of(width)
    bits = groups.bit_length() - 1
    cut = halved(pieces, parts)
    incoming = [[pltpu.VMEM((groups >> (b + 1),) + shape_sent(rows, size), bf16) for b in range(bits)] for _, size in cut]
    kinds = sorted({size for _, size in cut})
    outgoing = [[pltpu.VMEM((sum(size == kind for _, size in cut), groups >> (b + 1)) + shape_sent(rows, kind), bf16)
                 for b in range(bits)] for kind in kinds]
    straight = pltpu.VMEM((max(len(pieces) - len(cut), 1), groups - 1) + shape_sent(rows, pieces[-1][1]), bf16)
    split = hidden.reshape(-1, 2, rows, tokens)
    token_grads, weight_grad = pl.pallas_call(
        functools.partial(kernel, n_dp, n_mp),
        out_shape=(
            pltpu.VMEM((3 * width, tokens), bf16),
            pltpu.VMEM((3, rows, width), f32),
        ),
        in_specs=[anywhere] * 5,
        out_specs=(vmem, vmem),
        scratch_shapes=[
            pltpu.SMEM(helper.shape[:1], jnp.int32),
            pltpu.VMEM(segments.shape, jnp.int32),
            pltpu.VMEM(split.shape, bf16),
            pltpu.VMEM(qkv.shape, bf16),
            pltpu.VMEM(grad_attn.shape, bf16),
            pltpu.VMEM((3 * width, tokens), bf16),
            pltpu.VMEM((n_dp, 1, pair), jnp.int32),
            pltpu.VMEM((n_dp, 1, pair), jnp.int32),
            pltpu.VMEM((parts, n_dp, width // parts // 2, pair), bf16),
            [pltpu.VMEM((n_dp, width // parts // 2, pair), bf16) for _ in range(parts)],
            pltpu.VMEM((2, groups, rows, tokens), bf16),
            pltpu.VMEM((pairs * heads, pair, pair), f32),
            pltpu.VMEM((width, tokens), bf16),
            [pltpu.VMEM((groups, rows, size), f32) for _, size in pieces],
            outgoing,
            incoming,
            straight,
            straight,
            dma((5,)),
            dma, dma, dma((parts,)), dma((parts,)),
            dma, dma((5 if rows % 80 == 0 else 1,)), dma, dma, dma, dma, dma((2,)), dma((2,)), dma,
            dma, dma((len(pieces),)), dma((len(kinds), bits)), dma((len(cut), bits)),
            dma, dma,
        ],
        compiler_params=pltpu.CompilerParams(
            collective_id=0, has_side_effects=True, vmem_limit_bytes=65000000
        ),
    )(helper[:, 0], split, qkv, segments, grad_attn)
    token_grads, weight_grad = pl.pallas_call(
        write_out,
        out_shape=(
            jax.ShapeDtypeStruct(token_grads.shape, bf16),
            jax.ShapeDtypeStruct(weight_grad.shape, f32),
        ),
        in_specs=[vmem, vmem],
        out_specs=(anywhere, anywhere),
        scratch_shapes=[dma((2,))],
        compiler_params=pltpu.CompilerParams(vmem_limit_bytes=8 * 1024 * 1024),
    )(token_grads, weight_grad)
    return token_grads.reshape(qkv.shape), jnp.transpose(weight_grad, (1, 0, 2))


def solution(mesh):
    in_specs = (P("mp", "dp"), P(None, "mp", "dp"), P("dp", None), P("dp", None), P("mp", "dp"))
    out_specs = (P(None, "mp", "dp"), P("dp", None, "mp"))
    return jax.shard_map(
        functools.partial(per_device, mesh.shape["dp"], mesh.shape["mp"]),
        mesh=mesh, in_specs=in_specs, out_specs=out_specs, check_vma=False,
    )
```

```python
import functools
import math

import jax
import jax.numpy as jnp
from jax import lax
from jax.experimental import pallas as pl
from jax.experimental.pallas import tpu as pltpu
from jax.sharding import PartitionSpec as P

HEAD_DIM = 80
DIRECT_PIECES = 1
MESH = pl.DeviceIdType.MESH


def contract(a, b, dims):
    return lax.dot_general(a, b, (dims, ((), ())), preferred_element_type=jnp.float32)


def parts_of(width):
    return 2 if width // HEAD_DIM % 2 == 0 and width >= 256 else 1


def pieces_of(width):
    lanes, parts = 128, parts_of(width)
    if parts == 1:
        sizes = [3 * width % lanes] * (3 * width % lanes > 0) + [lanes] * (3 * width // lanes)
        out, high = [], 3 * width
        for size in sizes:
            high -= size
            out.append((high, size))
        return out
    upper, lower = [], []
    for j in (2, 1, 0):
        high = (j + 1) * width
        for i in range(width // parts // lanes):
            high -= lanes
            upper += [(high + lanes // 2, lanes // 2), (high, lanes // 2)] if j == 2 and i == 0 else [(high, lanes)]
        while high > j * width:
            size = min(lanes, high - j * width)
            high -= size
            lower.append((high, size))
    return upper + lower


def halved(pieces, parts):
    return pieces[:len(pieces) - DIRECT_PIECES] if parts > 1 else pieces


def shape_sent(rows, size):
    return (rows // 2, 2 * size) if 2 * size <= 128 and rows % 32 == 0 else (rows, size)


def kernel(n_dp, n_mp, helper_hbm, hid_hbm, qkv_hbm, seg_hbm, ga_hbm, tg_ref, wg_ref,
           helper_ref, seg_ref, hid_ref, qkv_ref, ga_ref, mate_tg,
           seg_send, seg_recv, ga_send, ga_recv, hid_all, prob_s, dout_s, acc, sends, recvs, straight_out, straight_in,
           load_sem, seg_ss, seg_rs, ga_ss, ga_rs, hx_ss, hx_rs, hz_ss, hz_rs, hy_ss, hy_rs, hp_ss, hp_rs, own_sem,
           tg_ss, tg_rs, st_ss, st_rs, di_ss, di_rs):
    d = lax.axis_index("dp")
    m = lax.axis_index("mp")
    y, c = m // 2, m % 2
    z, x = d // 2, d % 2
    far, groups = n_mp // 2, n_dp // 2
    win = seg_ref.shape[1]
    pair = 2 * win
    width, tokens = qkv_ref.shape[1], qkv_ref.shape[2]
    heads, pairs = width // HEAD_DIM, tokens // pair
    parts = parts_of(width)
    band = width // parts
    half = band // 2
    blocks, rows = hid_ref.shape[0], hid_ref.shape[2]
    scale = 1.0 / math.sqrt(HEAD_DIM)
    mate = 2 * y + 1 - c
    beside = 2 * z + 1 - x
    pieces = pieces_of(width)
    bits = groups.bit_length() - 1
    bf16, f32 = jnp.bfloat16, jnp.float32

    loads = [pltpu.make_async_copy(a, b, load_sem.at[i])
             for i, (a, b) in enumerate(((ga_hbm, ga_ref), (hid_hbm, hid_ref), (qkv_hbm, qkv_ref),
                                         (seg_hbm, seg_ref), (helper_hbm, helper_ref)))]
    for i in (0, 3, 1, 2, 4):
        loads[i].start()

    barrier = pltpu.get_barrier_semaphore()
    for k in range(1, n_dp):
        pl.semaphore_signal(barrier, inc=1, device_id={"dp": lax.rem(d + k, n_dp)}, device_id_type=MESH)
    for k in range(1, far):
        pl.semaphore_signal(barrier, inc=1, device_id={"mp": 2 * lax.rem(y + k, far) + c}, device_id_type=MESH)
    pl.semaphore_signal(barrier, inc=1, device_id={"mp": mate}, device_id_type=MESH)

    loads[0].wait()
    lane = lax.broadcasted_iota(jnp.int32, (half, pair), 1)
    low = lane < win
    for j in range(n_dp // 2):
        both = ga_ref[:, j * pair:(j + 1) * pair].astype(f32)
        for g in range(parts):
            top, bottom = both[g * band:g * band + half], both[g * band + half:(g + 1) * band]
            ga_send[g, 2 * j] = jnp.where(low, top, pltpu.roll(bottom, win, 1)).astype(bf16)
            ga_send[g, 2 * j + 1] = jnp.where(low, pltpu.roll(top, win, 1), bottom).astype(bf16)
    for g in range(parts):
        ga_recv[g][d] = ga_send[g, d]
    loads[3].wait()
    seg = seg_ref[...]
    seg_twice = jnp.concatenate([seg, seg], axis=1)
    for o in range(n_dp):
        seg_send[o] = seg_twice[o:o + 1]
    seg_recv[d] = seg_send[d]
    loads[1].wait()

    def seg_copy(k):
        to = lax.rem(d + k, n_dp)
        return pltpu.make_async_remote_copy(seg_send.at[to], seg_recv.at[d], seg_ss, seg_rs,
                                            device_id={"dp": to}, device_id_type=MESH)

    others = pl.ds(0, n_dp - 1)
    seg_all = pltpu.make_async_remote_copy(seg_send.at[others], seg_recv.at[others], seg_ss, seg_rs,
                                           device_id={"dp": beside}, device_id_type=MESH)

    def ga_copy(g, k):
        to = lax.rem(d + k, n_dp)
        return pltpu.make_async_remote_copy(ga_send.at[g, to], ga_recv[g].at[d], ga_ss.at[g], ga_rs.at[g],
                                            device_id={"dp": to}, device_id_type=MESH)

    def ga_all(g):
        return pltpu.make_async_remote_copy(ga_send.at[g, others], ga_recv[g].at[others], ga_ss.at[g], ga_rs.at[g],
                                            device_id={"dp": beside}, device_id_type=MESH)

    def hid_at(side, member):
        return hid_all.at[side, pl.ds(member * blocks, blocks)]

    own = pltpu.make_async_copy(hid_ref.at[:, x], hid_at(0, m), own_sem)
    chunks = 5 if rows % 80 == 0 else 1

    def hid_x(q):
        at = pl.ds(q * (rows // chunks), rows // chunks)
        return pltpu.make_async_remote_copy(hid_ref.at[:, 1 - x, at], hid_at(1, m).at[:, at], hx_ss, hx_rs.at[q],
                                            device_id={"dp": beside}, device_id_type=MESH)

    def pass_copy(q, k):
        at = pl.ds(q * (rows // chunks), rows // chunks)
        return pltpu.make_async_remote_copy(hid_at(1, m).at[:, at], hid_at(1, m).at[:, at], hz_ss, hz_rs,
                                            device_id={"mp": 2 * lax.rem(y + k, far) + c}, device_id_type=MESH)

    def hid_copy(k):
        return pltpu.make_async_remote_copy(hid_ref.at[:, x], hid_at(0, m), hy_ss, hy_rs,
                                            device_id={"mp": 2 * lax.rem(y + k, far) + c}, device_id_type=MESH)

    def mate_copy(side, k):
        at = hid_at(side, 2 * lax.rem(y - k + far, far) + c)
        src = hid_ref.at[:, x] if (side, k) == (0, 0) else at
        return pltpu.make_async_remote_copy(src, at, hp_ss.at[side], hp_rs.at[side],
                                            device_id={"mp": mate}, device_id_type=MESH)

    def members(side, count, send, recv):
        at = hid_all.at[side, pl.ds(0, count * blocks)]
        return pltpu.make_async_remote_copy(at, at, send, recv, device_id={"mp": mate}, device_id_type=MESH)

    pl.semaphore_wait(barrier, n_dp - 1 + far)
    for k in range(1, n_dp):
        seg_copy(k).start()
    for k in range(1, far):
        hid_copy(k).start()
    for k in sorted(range(1, n_dp), key=lambda k: (1 - k % 2, -min(k, n_dp - k))):
        ga_copy(parts - 1, k).start()
    for q in range(chunks):
        hid_x(q).start()
    mate_copy(0, 0).start()
    own.start()
    loads[2].wait()
    loads[4].wait()

    def at_of(p, h):
        return slice(h * HEAD_DIM, (h + 1) * HEAD_DIM), slice(p * pair, (p + 1) * pair)

    for p in range(pairs):
        for h in range(heads):
            at = at_of(p, h)
            prob_s[p * heads + h] = contract(qkv_ref[(1,) + at], qkv_ref[(0,) + at], ((0,), (0,))) * scale
    seg_all.wait()
    lane_row = lax.broadcasted_iota(jnp.int32, (1, pair), 1)
    for p in range(pairs):
        first, second = seg_recv[helper_ref[2 * p]], seg_recv[helper_ref[2 * p + 1]]
        name = jnp.where(lane_row < win, first, second + 2).astype(f32)
        across = jnp.broadcast_to(name, (pair, pair))
        same = across == across.T
        for h in range(heads):
            scores = jnp.where(same, prob_s[p * heads + h], -1e30)
            prob = jnp.exp(scores - jnp.max(scores, axis=0, keepdims=True))
            prob_s[p * heads + h] = prob / jnp.sum(prob, axis=0, keepdims=True)

    def pass_on(q):
        hid_x(q).wait_recv()
        for k in range(1, far):
            pass_copy(q, k).start()

    before = min(2, chunks)
    for q in range(before):
        pass_on(q)
    for g in range(parts - 1):
        for k in range(1, n_dp):
            ga_copy(g, k).start()

    def tg_copy(s):
        at = pl.ds(*pieces[s])
        return pltpu.make_async_remote_copy(tg_ref.at[at], mate_tg.at[at], tg_ss, tg_rs.at[s],
                                            device_id={"dp": beside}, device_id_type=MESH)

    def put(j, p, h, grads):
        tg_ref[j * width + h * HEAD_DIM:j * width + (h + 1) * HEAD_DIM, p * pair:(p + 1) * pair] = grads.astype(bf16)

    def dv(g, p):
        first = ga_recv[g][helper_ref[2 * p]].astype(f32)
        second = ga_recv[g][helper_ref[2 * p + 1]].astype(f32)
        top = jnp.where(low, first, pltpu.roll(second, win, 1))
        bottom = jnp.where(low, pltpu.roll(first, win, 1), second)
        dout_s[g * band:(g + 1) * band, p * pair:(p + 1) * pair] = jnp.concatenate([top, bottom], axis=0).astype(bf16)
        for h in range(g * heads // parts, (g + 1) * heads // parts):
            put(2, p, h, contract(dout_s[at_of(p, h)], prob_s[p * heads + h].astype(bf16), ((1,), (1,))))

    def attend(g, p):
        for h in range(g * heads // parts, (g + 1) * heads // parts):
            at = at_of(p, h)
            query, key, value = qkv_ref[(0,) + at], qkv_ref[(1,) + at], qkv_ref[(2,) + at]
            prob = prob_s[p * heads + h]
            dprob = contract(value, dout_s[at], ((0,), (0,)))
            delta = jnp.sum(prob.astype(bf16).astype(f32) * dprob, axis=0, keepdims=True)
            dscore = (prob * (dprob - delta)).astype(bf16)
            put(0, p, h, contract(key, dscore, ((1,), (0,))) * scale)
            put(1, p, h, contract(query, dscore, ((1,), (1,))) * scale)

    sent = []

    def send_ready(g, j):
        for s, (start, size) in enumerate(pieces):
            if s not in sent and start // width >= j and (start % width >= g * band or parts == 1 or g == 0):
                if start // width == 2 or j < 2:
                    tg_copy(s).start()
                    sent.append(s)

    later = max(before, chunks - 1)
    for g in reversed(range(parts)):
        ga_all(g).wait()
        for p in range(pairs):
            dv(g, p)
        send_ready(g, 2)
        if g == parts - 1:
            for q in range(before, later):
                pass_on(q)
            members(0, far - 1, hy_ss, hy_rs).wait()
            for k in range(1, far):
                mate_copy(0, k).start()
        for p in range(pairs if g > 0 else 0):
            if p == 1:
                for q in range(later, chunks):
                    pass_on(q)
                mate_copy(1, 0).start()
            attend(g, p)
        if g > 0:
            send_ready(g, 0)
    if parts == 1:
        mate_copy(1, 0).start()
    members(1, far - 1, hz_ss, hz_rs).wait()
    for k in range(1, far):
        mate_copy(1, k).start()
    own.wait()
    members(0, far, hp_ss.at[0], hp_rs.at[0]).wait()

    def products(side, of, s, blocks):
        at = slice(pieces[s][0], pieces[s][0] + pieces[s][1])
        if rows % 16 == 0:
            stacked = jnp.concatenate([hid_all[side, t] for t in blocks], axis=0)
            return contract(stacked, of[at], ((1,), (1,))).reshape(len(blocks), rows, pieces[s][1])
        return [contract(hid_all[side, t], of[at], ((1,), (1,))) for t in blocks]

    def mine(s):
        for t, block in enumerate(products(0, tg_ref, s, range(groups))):
            acc[s][t] = block

    def theirs(s, blocks):
        for t, block in zip(blocks, products(1, mate_tg, s, blocks)):
            acc[s][t] = acc[s][t] + block

    def packed(block):
        if block.shape[1] * 2 <= 128 and rows % 32 == 0:
            block = jnp.concatenate([block[:rows // 2], block[rows // 2:]], axis=1)
        return block.astype(bf16)

    def unpacked(block, size):
        block = block.astype(f32)
        if block.shape[1] != size:
            block = jnp.concatenate([block[:, :size], block[:, size:]], axis=0)
        return block

    def finish(s, total):
        start, size = pieces[s]
        for j in range(3):
            a, b = max(start, j * width), min(start + size, (j + 1) * width)
            if a < b:
                wg_ref[j, :, a - j * width:b - j * width] = total[:, a - start:b - start]

    count = len(pieces)
    straight = len(halved(pieces, parts))
    kinds = sorted({size for _, size in pieces[:straight]})
    place = [(kinds.index(size), sum(other == size for _, other in pieces[:s])) for s, (_, size) in enumerate(pieces[:straight])]

    def outgoing(s, b):
        kind, at = place[s]
        return sends[kind][b].at[at]

    def half_copy(s, b):
        bit = z // 2 ** b % 2
        to = z + (1 - 2 * bit) * 2 ** b
        return pltpu.make_async_remote_copy(outgoing(s, b), recvs[s][b], st_ss.at[place[s][0], b], st_rs.at[s, b],
                                            device_id={"dp": 2 * to + x}, device_id_type=MESH)

    def begin(s, b):
        bit = z // 2 ** b % 2
        for i in range(groups >> (b + 1)):
            t = z % 2 ** b + (1 - bit) * 2 ** b + i * 2 ** (b + 1)
            outgoing(s, b)[i] = packed(acc[s][t])
        half_copy(s, b).start()

    def end(s, b):
        half_copy(s, b).wait_recv()
        bit = z // 2 ** b % 2
        for i in range(groups >> (b + 1)):
            t = z % 2 ** b + bit * 2 ** b + i * 2 ** (b + 1)
            acc[s][t] = acc[s][t] + unpacked(recvs[s][b][i], pieces[s][1])

    def direct_copy(s, k):
        return pltpu.make_async_remote_copy(straight_out.at[s, k - 1], straight_in.at[s, k - 1], di_ss, di_rs,
                                            device_id={"dp": 2 * lax.rem(z + k, groups) + x}, device_id_type=MESH)

    def advance(s, b):
        if 0 <= s < straight:
            end(s, b)
            if b + 1 < bits:
                begin(s, b + 1)
            else:
                finish(s, acc[s][z])

    swapped = groups == 4
    inner = z == 2
    ahead = 2 if parts > 1 else 0
    attends = {3: range(pairs // 2), 4: range(pairs // 2, pairs)} if parts > 1 else {0: range(pairs)}
    for s in range(ahead):
        mine(s)
    members(1, far, hp_ss.at[1], hp_rs.at[1]).wait()
    bit = z % 2
    sent_first = [1 - bit + 2 * i for i in range(groups // 2)]
    kept = [bit + 2 * i for i in range(groups // 2)]
    for turn in range(count + 2 + 4 * (bits - 1)):
        for p in attends.get(turn, ()):
            attend(0, p)
        if turn == max(attends):
            send_ready(0, 0)
        if turn < count:
            if turn >= ahead:
                mine(turn)
            tg_copy(turn).wait_recv()
            if turn < straight:
                theirs(turn, sent_first)
                if swapped:
                    pl.when(inner)(functools.partial(advance, turn - 2, 0))
                begin(turn, 0)
                theirs(turn, kept)
            else:
                theirs(turn, range(groups))
                for i in range(groups - 1):
                    t = i + (i >= z).astype(jnp.int32)
                    k = lax.rem(t - z + groups, groups)
                    straight_out[turn - straight, k - 1] = packed(acc[turn][t])
                    direct_copy(turn - straight, k).start()
        for b in range(bits):
            step = functools.partial(advance, turn - 2 - 3 * b, b)
            if swapped and b == 0 and turn < straight:
                pl.when(jnp.logical_not(inner))(step)
            else:
                step()
    if straight < count:
        pltpu.make_async_remote_copy(straight_out, straight_in, di_ss, di_rs,
                                     device_id={"dp": beside}, device_id_type=MESH).wait()
    for s in range(straight, count):
        total = acc[s][z]
        for k in range(1, groups):
            total = total + unpacked(straight_in[s - straight, k - 1], pieces[s][1])
        finish(s, total)
    pltpu.make_async_remote_copy(tg_ref, mate_tg, tg_ss, tg_rs.at[0],
                                 device_id={"dp": beside}, device_id_type=MESH).wait_send()
    pltpu.make_async_remote_copy(hid_ref.at[:, 1 - x], hid_at(1, m), hx_ss, hx_rs.at[0],
                                 device_id={"dp": beside}, device_id_type=MESH).wait_send()
    for kind in range(len(kinds)):
        for b in range(bits):
            pltpu.make_async_remote_copy(sends[kind][b], sends[kind][b], st_ss.at[kind, b], st_rs.at[0, b],
                                         device_id={"dp": beside}, device_id_type=MESH).wait_send()


def write_out(tg_ref, wg_ref, tg_hbm, wg_hbm, sems):
    copies = [pltpu.make_async_copy(tg_ref, tg_hbm, sems.at[0]), pltpu.make_async_copy(wg_ref, wg_hbm, sems.at[1])]
    for copy in copies:
        copy.start()
    for copy in copies:
        copy.wait()


def per_device(n_dp, n_mp, hidden, qkv, helper, segments, grad_attn):
    width, tokens = qkv.shape[1], qkv.shape[2]
    rows = hidden.shape[0] * n_mp // n_dp
    win = segments.shape[1]
    pair = 2 * win
    parts = parts_of(width)
    heads, pairs, groups, far = width // HEAD_DIM, tokens // pair, n_dp // 2, n_mp // 2
    bf16, f32 = jnp.bfloat16, jnp.float32
    vmem, anywhere = pl.BlockSpec(memory_space=pltpu.VMEM), pl.BlockSpec(memory_space=pltpu.HBM)
    dma = pltpu.SemaphoreType.DMA
    pieces = pieces_of(width)
    bits = groups.bit_length() - 1
    cut = halved(pieces, parts)
    incoming = [[pltpu.VMEM((groups >> (b + 1),) + shape_sent(rows, size), bf16) for b in range(bits)] for _, size in cut]
    kinds = sorted({size for _, size in cut})
    outgoing = [[pltpu.VMEM((sum(size == kind for _, size in cut), groups >> (b + 1)) + shape_sent(rows, kind), bf16)
                 for b in range(bits)] for kind in kinds]
    straight = pltpu.VMEM((max(len(pieces) - len(cut), 1), groups - 1) + shape_sent(rows, pieces[-1][1]), bf16)
    split = hidden.reshape(-1, 2, rows, tokens)
    token_grads, weight_grad = pl.pallas_call(
        functools.partial(kernel, n_dp, n_mp),
        out_shape=(
            pltpu.VMEM((3 * width, tokens), bf16),
            pltpu.VMEM((3, rows, width), f32),
        ),
        in_specs=[anywhere] * 5,
        out_specs=(vmem, vmem),
        scratch_shapes=[
            pltpu.SMEM(helper.shape[:1], jnp.int32),
            pltpu.VMEM(segments.shape, jnp.int32),
            pltpu.VMEM(split.shape, bf16),
            pltpu.VMEM(qkv.shape, bf16),
            pltpu.VMEM(grad_attn.shape, bf16),
            pltpu.VMEM((3 * width, tokens), bf16),
            pltpu.VMEM((n_dp, 1, pair), jnp.int32),
            pltpu.VMEM((n_dp, 1, pair), jnp.int32),
            pltpu.VMEM((parts, n_dp, width // parts // 2, pair), bf16),
            [pltpu.VMEM((n_dp, width // parts // 2, pair), bf16) for _ in range(parts)],
            pltpu.VMEM((2, groups, rows, tokens), bf16),
            pltpu.VMEM((pairs * heads, pair, pair), f32),
            pltpu.VMEM((width, tokens), bf16),
            [pltpu.VMEM((groups, rows, size), f32) for _, size in pieces],
            outgoing,
            incoming,
            straight,
            straight,
            dma((5,)),
            dma, dma, dma((parts,)), dma((parts,)),
            dma, dma((5 if rows % 80 == 0 else 1,)), dma, dma, dma, dma, dma((2,)), dma((2,)), dma,
            dma, dma((len(pieces),)), dma((len(kinds), bits)), dma((len(cut), bits)),
            dma, dma,
        ],
        compiler_params=pltpu.CompilerParams(
            collective_id=0, has_side_effects=True, vmem_limit_bytes=65000000
        ),
    )(helper[:, 0], split, qkv, segments, grad_attn)
    token_grads, weight_grad = pl.pallas_call(
        write_out,
        out_shape=(
            jax.ShapeDtypeStruct(token_grads.shape, bf16),
            jax.ShapeDtypeStruct(weight_grad.shape, f32),
        ),
        in_specs=[vmem, vmem],
        out_specs=(anywhere, anywhere),
        scratch_shapes=[dma((2,))],
        compiler_params=pltpu.CompilerParams(vmem_limit_bytes=8 * 1024 * 1024),
    )(token_grads, weight_grad)
    return token_grads.reshape(qkv.shape), jnp.transpose(weight_grad, (1, 0, 2))


def solution(mesh):
    in_specs = (P("mp", "dp"), P(None, "mp", "dp"), P("dp", None), P("dp", None), P("mp", "dp"))
    out_specs = (P(None, "mp", "dp"), P("dp", None, "mp"))
    return jax.shard_map(
        functools.partial(per_device, mesh.shape["dp"], mesh.shape["mp"]),
        mesh=mesh, in_specs=in_specs, out_specs=out_specs, check_vma=False,
    )
```
